32 devices in a mesh: seq: 2 (over y), row: 4 (over z), col: 4 (over x, core).
Axes of the slice: x: 2, y: 2, z: 4, core: 2. Of those that a mesh axis runs over, the one named last changes fastest.
Arguments:
- stream: bfloat16 [3072, 3072], P(('seq', 'row'), 'col'), may hold values from -6 to 6
- query_input: bfloat16 [3072, 3072], P(('seq', 'row'), 'col'), may hold values from -400 to 400
- key_input: bfloat16 [3072, 3072], P(('seq', 'row'), 'col'), may hold values from -400 to 400
- value_input: bfloat16 [3072, 3072], P(('seq', 'row'), 'col'), may hold values from -6 to 6
- q_gain: float32 [24, 128], P('col'), may hold values from 0.5 to 7
- k_gain: float32 [24, 128], P('col'), may hold values from 0.5 to 7
- out_weight: bfloat16 [3072, 3072], P('row', 'col'), may hold values from -0.109375 to 0.109375
- gate: float32 [3072], P('col'), may hold values from -4 to 4
Outputs:
- out: bfloat16 [3072, 3072], P(('seq', 'row'), 'col')
The draws below stay inside these ranges and needn't reach their ends.
All inputs are finite; a program needn't handle non-finite values.
Results may differ from the reference program's by a relative error of at most 0.0057.
Values may be sent and summed in bfloat16 or wider, within the bound.
No kernel may reach another device: no remote copies, remote signals or barrier semaphores. Data moves between devices by JAX's collectives and lax.ppermute only.
A program may use at most 64 MiB of HBM per device.

```python
import math
import jax
import jax.numpy as jnp
from jax import lax

D = 3072
HEADS = 24
HD = 128
TILE = 384
WTILES = 1
TTILES = 2
HTILES = 4
TOKENS = 3072


def column_profile(key, member):
    return jnp.exp(jax.random.uniform(jax.random.fold_in(key, member), (D,), jnp.float32, 0.0, math.log(3.0)))


def projected_draw(key, member):
    row_scales = jnp.exp(jax.random.uniform(jax.random.fold_in(key, member + 100), (TOKENS, 1), jnp.float32, 0.0, math.log(10.0)))
    gaussian = jax.random.truncated_normal(jax.random.fold_in(key, member + 200), -4.0, 4.0, (TOKENS, D), jnp.float32)
    return (gaussian * row_scales * column_profile(key, member)[None, :]).astype(jnp.bfloat16)


def gain_draw(key, member):
    return jnp.exp(jax.random.uniform(jax.random.fold_in(key, member + 300), (HEADS, HD), jnp.float32, 0.0, math.log(3.0)))


def draw_query_input(key, part):
    return projected_draw(key, 1)


def draw_key_input(key, part):
    return projected_draw(key, 2)


def draw_q_gain(key, part):
    return gain_draw(key, 1)


def draw_k_gain(key, part):
    return gain_draw(key, 2)


def block_scale(key, dims, cuts, smallest, high):
    def one(position, blocks):
        draws = jax.random.uniform(jax.random.fold_in(jax.random.fold_in(key, 6), position), (blocks,), jnp.float32, smallest / len(cuts), high / len(cuts))
        return jnp.repeat(jnp.exp(draws), dims[position] // blocks).reshape((-1,) + (1,) * (len(dims) - position - 1))

    factor_of = one(*cuts[0])
    for cut in cuts[1:]:
        factor_of = factor_of * one(*cut)
    return factor_of


def bell_draw(stream_key, shape, deviation, reach, shards=(), held_as=jnp.bfloat16):
    drawn = jax.random.normal(stream_key, shape, jnp.float32) * deviation
    if len(shards) > 0:
        drawn = block_scale(stream_key, shape, shards, -0.22, 0.18) * drawn
    return jnp.clip(drawn, min=-reach, max=reach).astype(held_as)


def setup_inputs(seed: int = 0) -> dict:
    splits = jax.random.split(jax.random.key(seed), 9)
    stream = bell_draw(splits[0], (TOKENS, D), 1.0, 6.0, ((0, 8), (1, 4)))
    query_input = draw_query_input(jax.random.fold_in(splits[8], 71), 0)
    key_input = draw_key_input(jax.random.fold_in(splits[8], 71), 0)
    value_input = bell_draw(splits[3], (TOKENS, D), 1.0, 6.0, ((0, 8), (1, 4)))
    q_gain = draw_q_gain(jax.random.fold_in(splits[8], 71), 0)
    k_gain = draw_k_gain(jax.random.fold_in(splits[8], 71), 0)
    out_weight = bell_draw(splits[6], (D, D), D ** -0.5, 0.109375, ((0, 4), (1, 4)))
    gate = bell_draw(splits[7], (D,), 1.0, 4.0, ((0, 4),), jnp.float32)
    return dict(stream=stream, query_input=query_input, key_input=key_input, value_input=value_input, q_gain=q_gain, k_gain=k_gain, out_weight=out_weight, gate=gate)


EPSILON = 1e-06
NEGATIVE_FLOOR = -1e+30

def normalize(values, gain_table):
    token_count = values.shape[0]
    head_count, head_size = gain_table.shape
    split = values.astype(jnp.float32).reshape(token_count, head_count, head_size)
    mean_square = lax.optimization_barrier(jnp.mean(split * split, axis=-1, keepdims=True))
    return (split * lax.rsqrt(mean_square + EPSILON) * gain_table).astype(jnp.bfloat16)

def combine(maxima, layer_sums, weighted, presence):
    mask = presence[:, None, None]
    maxima = jnp.where(mask, maxima, NEGATIVE_FLOOR)
    layer_sums = jnp.where(mask, layer_sums, 0.0)
    overall = lax.optimization_barrier(jnp.max(maxima, axis=0))
    factors = jnp.exp(maxima - overall)
    denominator = lax.optimization_barrier(jnp.sum(factors * layer_sums, axis=0))
    numerator = lax.optimization_barrier(jnp.sum(jnp.transpose(factors, (0, 2, 1))[..., None] * weighted, axis=0))
    return numerator / jnp.transpose(denominator)[..., None]

def reference(stream, query_input, key_input, value_input, q_gain, k_gain, out_weight, gate):
    block_size = WTILES * TILE
    score_scale = 1.0 / math.sqrt(HD)
    grid_shape = (TTILES, HTILES, block_size, HEADS, HD)
    queries = lax.optimization_barrier(normalize(query_input, q_gain)).reshape(grid_shape)
    normed_keys = lax.optimization_barrier(normalize(key_input, k_gain)).reshape(grid_shape)
    value_grid = value_input.reshape(grid_shape)

    def one_block(block_index):
        time_slot = block_index // HTILES
        height_slot = block_index % HTILES
        query_block = queries[time_slot, height_slot].astype(jnp.float32)
        maxima = []
        layer_sums = []
        weighted_list = []
        presence = []
        for offset_time in (-1, 0, 1):
            for offset_height in (-1, 0, 1):
                source_time = jnp.clip(time_slot + offset_time, 0, TTILES - 1)
                source_height = jnp.clip(height_slot + offset_height, 0, HTILES - 1)
                key_block = normed_keys[source_time, source_height].astype(jnp.float32)
                value_block = value_grid[source_time, source_height].astype(jnp.float32)
                scores = jnp.einsum('qhd,khd->hqk', query_block, key_block) * score_scale
                layer_max = lax.optimization_barrier(jnp.max(scores, axis=-1))
                unnormed = lax.optimization_barrier(jnp.exp(scores - layer_max[..., None]).astype(jnp.bfloat16)).astype(jnp.float32)
                layer_sums.append(lax.optimization_barrier(jnp.sum(unnormed, axis=-1)))
                weighted_list.append(jnp.einsum('hqk,khd->qhd', unnormed, value_block))
                maxima.append(layer_max)
                inside_time = (time_slot + offset_time >= 0) & (time_slot + offset_time < TTILES)
                inside_height = (height_slot + offset_height >= 0) & (height_slot + offset_height < HTILES)
                presence.append(inside_time & inside_height)
        merged = combine(jnp.stack(maxima), jnp.stack(layer_sums), jnp.stack(weighted_list), jnp.stack(presence))
        return merged.reshape(block_size, D).astype(jnp.bfloat16)
    blocks = lax.map(one_block, jnp.arange(TTILES * HTILES, dtype=jnp.int32))
    attention = blocks.reshape(TOKENS, D)
    projected = jnp.dot(attention, out_weight, preferred_element_type=jnp.float32)
    return (stream.astype(jnp.float32) + gate * projected).astype(jnp.bfloat16)
```

```python
import functools
import math

import jax
import jax.numpy as jnp
from jax import lax
from jax.experimental import pallas as pl
from jax.experimental.pallas import tpu as pltpu
from jax.sharding import PartitionSpec as P

EPSILON = 1e-06
NEGATIVE_FLOOR = -1e30


def padded_2(block, sides, width):
    for axis, dim in sides:
        count = lax.axis_size(axis)
        forward = [(i, i + 1) for i in range(count - 1)]
        backward = [(target, source) for source, target in forward]
        low = lax.ppermute(
            lax.slice_in_dim(block, block.shape[dim] - width, None, axis=dim), axis, forward
        )
        high = lax.ppermute(lax.slice_in_dim(block, 0, width, axis=dim), axis, backward)
        block = jnp.concatenate([low, block, high], axis=dim)
    return block


def normalize(values, gain_table):
    token_count = values.shape[0]
    head_count, head_size = gain_table.shape
    split = values.astype(jnp.float32).reshape(token_count, head_count, head_size)
    mean_square = jnp.mean(split * split, axis=-1, keepdims=True)
    return (split * lax.rsqrt(mean_square + EPSILON) * gain_table).astype(jnp.bfloat16)


def layer_terms(queries, key_rows, value_rows, score_scale):
    scores = (
        jnp.einsum("qhd,khd->hqk", queries, key_rows, preferred_element_type=jnp.float32)
        * score_scale
    )
    layer_max = jnp.max(scores, axis=-1)
    unnormed = jnp.exp(scores - layer_max[..., None]).astype(jnp.bfloat16)
    layer_sum = jnp.sum(unnormed.astype(jnp.float32), axis=-1)
    weighted = jnp.einsum("hqk,khd->qhd", unnormed, value_rows, preferred_element_type=jnp.float32)
    return (layer_max, layer_sum, weighted)


def combine(maxima, layer_sums, weighted, presence):
    mask = presence[:, None, None]
    maxima = jnp.where(mask, maxima, NEGATIVE_FLOOR)
    layer_sums = jnp.where(mask, layer_sums, 0.0)
    overall = jnp.max(maxima, axis=0)
    factors = jnp.exp(maxima - overall)
    denominator = jnp.sum(factors * layer_sums, axis=0)
    numerator = jnp.sum(jnp.transpose(factors, (0, 2, 1))[..., None] * weighted, axis=0)
    return numerator / jnp.transpose(denominator)[..., None]


def body(stream, query_input, key_input, value_input, q_gain, k_gain, out_weight, gate):
    token_count, feature_count = query_input.shape
    head_count, head_size = q_gain.shape
    score_scale = 1.0 / math.sqrt(head_size)
    queries = normalize(query_input, q_gain)
    normed_keys = normalize(key_input, k_gain).reshape(token_count, feature_count)
    layered = jnp.stack([normed_keys, value_input], axis=0)[None, None]
    padded = padded_2(layered, (("seq", 0), ("row", 1)), 1)
    padded = padded.reshape(9, 2, token_count, feature_count)
    key_stack = padded[:, 0].reshape(9, token_count, head_count, head_size)
    value_stack = padded[:, 1].reshape(9, token_count, head_count, head_size)
    time_index = lax.axis_index("seq")
    time_count = lax.axis_size("seq")
    height_index = lax.axis_index("row")
    height_count = lax.axis_size("row")
    time_present = [time_index > 0, time_index >= 0, time_index < time_count - 1]
    height_present = [height_index > 0, height_index >= 0, height_index < height_count - 1]
    presence = jnp.stack(
        [time_flag & height_flag for time_flag in time_present for height_flag in height_present]
    )
    result_set = [
        layer_terms(queries, key_stack[layer_index], value_stack[layer_index], score_scale)
        for layer_index in range(9)
    ]
    maxima = jnp.stack([entry[0] for entry in result_set])
    layer_sums = jnp.stack([entry[1] for entry in result_set])
    weighted = jnp.stack([entry[2] for entry in result_set])
    attention = (
        combine(maxima, layer_sums, weighted, presence)
        .reshape(token_count, feature_count)
        .astype(jnp.bfloat16)
    )
    all_heads = lax.all_gather(attention, "col", axis=1, tiled=True)
    projected = jnp.dot(
        all_heads,
        lax.all_gather(out_weight, "row", axis=0, tiled=True),
        preferred_element_type=jnp.float32,
    )
    return (stream.astype(jnp.float32) + gate * projected).astype(jnp.bfloat16)


ABSENT = 1e30
LOG2_E = 1.4426950408889634
MIB = 1 << 20


def prep_kernel(time_ref, q_ref, k_ref, v_ref, qg_ref, kg_ref, q_keep, q_send, kv_keep, k_send, v_send):
    mine = time_ref[0]
    half = q_keep.shape[1]
    head_size = qg_ref.shape[1]
    count = half // head_size

    def normed(ref, gain_ref, part, index):
        start = pl.multiple_of(part * half + index * head_size, head_size)
        x = ref[:, pl.ds(start, head_size)].astype(jnp.float32)
        mean_square = jnp.mean(x * x, axis=-1, keepdims=True)
        gain = gain_ref[pl.ds(part * count + index, 1), :]
        return (x * lax.rsqrt(mean_square + EPSILON) * gain).astype(jnp.bfloat16)

    for part, k_out, v_out, q_out in (
        (1 - mine, k_send, v_send, q_send),
        (mine, kv_keep.at[0], kv_keep.at[1], q_keep),
    ):
        v_out[...] = v_ref[:, pl.ds(pl.multiple_of(part * half, half), half)]
        for index in range(count):
            columns = pl.ds(index * head_size, head_size)
            k_out[:, columns] = normed(k_ref, kg_ref, part, index)
            q_out[:, columns] = normed(q_ref, qg_ref, part, index)


def whole_spec(ndim):
    return pl.BlockSpec(memory_space=pltpu.VMEM)


def prep(mine, q, k, v, q_gain, k_gain):
    rows, width = q.shape
    half = width // 2
    one = jax.ShapeDtypeStruct((rows, half), jnp.bfloat16)
    two = jax.ShapeDtypeStruct((2, rows, half), jnp.bfloat16)
    return pl.pallas_call(
        prep_kernel,
        out_shape=[one, one, two, one, one],
        in_specs=[pl.BlockSpec(memory_space=pltpu.SMEM)] + [pl.BlockSpec(memory_space=pltpu.VMEM)] * 5,
        out_specs=[pl.BlockSpec(memory_space=pltpu.VMEM)] * 5,
        compiler_params=pltpu.CompilerParams(vmem_limit_bytes=16 * MIB),
        cost_estimate=pl.CostEstimate(flops=rows * width * 16, bytes_accessed=rows * width * 12, transcendentals=0),
    )(mine, q, k, v, q_gain, k_gain)


def attend_kernel(scale, first, last, *refs):
    present, q_mine, q_peer, k0, k1, k2, v0, v1, v2 = refs[:9]
    refs = refs[9:]
    if not first:
        m_in, acc_in = refs[:2]
        refs = refs[2:]
    flags = [None, present[0] > 0, present[1] > 0]
    keys = [k0[...], k1[...], k2[...]]
    size = keys[0].shape[1]
    ones = jnp.ones(keys[0].shape, jnp.bfloat16)
    values = [jnp.concatenate([v[...], ones], axis=1) for v in (v0, v1, v2)]
    factor = scale * LOG2_E
    for which, q_ref in enumerate((q_mine, q_peer)):
        q = q_ref[...]
        scores = [
            lax.dot_general(q, key, (((1,), (1,)), ((), ())), preferred_element_type=jnp.float32)
            for key in keys
        ]
        top = None
        for flag, score in zip(flags, scores):
            part = score[:, :size]
            for start in range(size, score.shape[1], size):
                part = jnp.maximum(part, score[:, start : start + size])
            if flag is not None:
                part = jnp.where(flag, part, NEGATIVE_FLOOR)
            top = part if top is None else jnp.maximum(top, part)
        top = jnp.max(top, axis=1, keepdims=True)
        if first:
            total = None
        else:
            before = m_in[which]
            top = jnp.maximum(before[:, :1], top)
            total = acc_in[which] * jnp.exp2((before[:, :1] - top) * factor)
        for flag, score, value in zip(flags, scores, values):
            shift = top if flag is None else jnp.where(flag, top, ABSENT)
            weights = jnp.exp2((score - shift) * factor).astype(jnp.bfloat16)
            term = jnp.dot(weights, value, preferred_element_type=jnp.float32)
            total = term if total is None else total + term
        if last:
            (out,) = refs
            out[which] = (total[:, :size] / total[:, size:]).astype(jnp.bfloat16)
        else:
            m_out, acc_out = refs
            m_out[which] = jnp.broadcast_to(top, (top.shape[0], size))
            acc_out[which] = total


def attend(present, q_mine, q_peer, keys, values, head_size, carry=None):
    rows, width = q_mine.shape
    heads = width // head_size
    column = pl.BlockSpec((rows, head_size), lambda h: (0, h))

    def spec(pair):
        array, part = pair
        if part is None:
            return column
        return pl.BlockSpec((None, rows, head_size), lambda h, part=part: (part, 0, h))

    m_spec = pl.BlockSpec((None, 2, rows, head_size), lambda h: (h, 0, 0, 0))
    acc_spec = pl.BlockSpec((None, 2, rows, 2 * head_size), lambda h: (h, 0, 0, 0))
    operands = list(keys) + list(values)
    in_specs = [pl.BlockSpec(memory_space=pltpu.SMEM), column, column] + [spec(pair) for pair in operands]
    arguments = [present, q_mine, q_peer] + [pair[0] for pair in operands]
    first, last = carry is None, carry is not None
    if first:
        out_shape = [
            jax.ShapeDtypeStruct((heads, 2, rows, head_size), jnp.float32),
            jax.ShapeDtypeStruct((heads, 2, rows, 2 * head_size), jnp.float32),
        ]
        out_specs = [m_spec, acc_spec]
    else:
        in_specs += [m_spec, acc_spec]
        arguments += list(carry)
        out_shape = jax.ShapeDtypeStruct((2, rows, width), jnp.bfloat16)
        out_specs = pl.BlockSpec((2, rows, head_size), lambda h: (0, 0, h))
    return pl.pallas_call(
        functools.partial(attend_kernel, 1.0 / math.sqrt(head_size), first, last),
        grid=(heads,),
        out_shape=out_shape,
        in_specs=in_specs,
        out_specs=out_specs,
        compiler_params=pltpu.CompilerParams(vmem_limit_bytes=40 * MIB),
        cost_estimate=pl.CostEstimate(
            flops=heads * 2 * rows * 3 * rows * head_size * 8,
            bytes_accessed=8 * MIB,
            transcendentals=heads * 2 * rows * 3 * rows,
        ),
    )(*arguments)


def project_kernel(shift_ref, a0, a1, w0, w1, w2, w3, w4, out):
    shift = shift_ref[0]
    for case in range(4):

        @pl.when(shift == case)
        def _(case=case):
            weights = [w0[...], w1[...], w2[...], w3[...] + w4[...]]
            pieces = [a0[0], a1[0], a0[1], a1[1]]
            total = None
            for index, piece in enumerate(pieces):
                term = jnp.dot(piece, weights[index ^ case], preferred_element_type=jnp.float32)
                total = term if total is None else total + term
            out[...] = total.astype(out.dtype)


def project(shift, pieces, weights, token_block, dtype):
    rows, width = pieces[0].shape[2:]
    columns = weights[0].shape[1]
    piece = pl.BlockSpec((2, None, rows, width), lambda i: (0, token_block, 0, 0))
    whole = pl.BlockSpec((width, columns), lambda i: (0, 0))
    return pl.pallas_call(
        project_kernel,
        grid=(1,),
        out_shape=jax.ShapeDtypeStruct((rows, columns), dtype),
        in_specs=[pl.BlockSpec(memory_space=pltpu.SMEM), piece, piece] + [whole] * 5,
        out_specs=pl.BlockSpec((rows, columns), lambda i: (0, 0)),
        compiler_params=pltpu.CompilerParams(vmem_limit_bytes=24 * MIB),
        cost_estimate=pl.CostEstimate(
            flops=rows * width * columns * 8, bytes_accessed=5 * MIB, transcendentals=0
        ),
    )(shift, *pieces, *weights)


def pair_body(stream, query_input, key_input, value_input, q_gain, k_gain, out_weight, gate):
    head_size = q_gain.shape[1]
    time = lax.axis_index("seq")
    height = lax.axis_index("row")
    column = lax.axis_index("col")
    rows = lax.axis_size("row")

    def swap(x):
        return lax.ppermute(x, "seq", [(0, 1), (1, 0)])

    def up(x):
        return lax.ppermute(x, "row", [(i, i + 1) for i in range(rows - 1)])

    def down(x):
        return lax.ppermute(x, "row", [(i + 1, i) for i in range(rows - 1)])

    def along(x, axis, mask):
        return lax.ppermute(x, axis, [(i, i ^ mask) for i in range(4)])

    one = lambda value: jnp.reshape(value, (1,)).astype(jnp.int32)
    q_keep, q_send, kv_keep, k_send, v_send = prep(
        one(time), query_input, key_input, value_input, q_gain, k_gain
    )
    k_peer = swap(k_send)
    v_peer = swap(v_send)
    q_peer = swap(q_send)
    kv_low, kv_high = up(kv_keep), down(kv_keep)
    k_low, k_high = up(k_peer), down(k_peer)
    v_low, v_high = up(v_peer), down(v_peer)

    present = jnp.stack([height > 0, height < rows - 1]).astype(jnp.int32)
    carry = attend(
        present, q_keep, q_peer,
        [(kv_keep, 0), (kv_low, 0), (kv_high, 0)], [(kv_keep, 1), (kv_low, 1), (kv_high, 1)],
        head_size,
    )
    attention = attend(
        present, q_keep, q_peer,
        [(k_peer, None), (k_low, None), (k_high, None)], [(v_peer, None), (v_low, None), (v_high, None)],
        head_size, carry,
    )

    depth = out_weight.shape[0] // 2
    mine = lax.dynamic_slice_in_dim(out_weight, time * depth, depth, axis=0)
    parts = 2
    width = out_weight.shape[1] // parts
    weights = []
    for part in range(parts):
        w0 = mine[:, part * width : (part + 1) * width]
        w1 = along(w0, "row", 1)
        w2 = along(w0, "row", 2)
        w3 = lax.ppermute(w0, "row", [(1, 2), (2, 1)])
        w4 = lax.ppermute(w2, "row", [(1, 0), (2, 3)])
        weights.append((w0, w1, w2, w3, w4))

    across = along(attention, "col", 2)
    near = jnp.stack([attention, across])
    far = along(near, "col", 1)
    shift = one(height ^ column)
    outs = []
    for part in range(parts):
        sent = project(shift, (near, far), weights[part], 1, jnp.bfloat16)
        outs.append(swap(sent))
    result = []
    for part in range(parts):
        own = project(shift, (near, far), weights[part], 0, jnp.float32)
        span = slice(part * width, (part + 1) * width)
        total = own + outs[part].astype(jnp.float32)
        result.append((stream[:, span].astype(jnp.float32) + gate[span] * total).astype(jnp.bfloat16))
    return jnp.concatenate(result, axis=1)


def solution(mesh):
    placed = (
        P(("seq", "row"), "col"),
        P(("seq", "row"), "col"),
        P(("seq", "row"), "col"),
        P(("seq", "row"), "col"),
        P("col", None),
        P("col", None),
        P("row", "col"),
        P("col"),
    )
    shape = mesh.shape
    paired = shape["seq"] == 2 and shape["row"] == 4 and shape["col"] == 4
    return jax.shard_map(
        pair_body if paired else body, mesh=mesh, in_specs=placed, out_specs=P(("seq", "row"), "col"), check_vma=False
    )
```

```python
import functools
import math

import jax
import jax.numpy as jnp
from jax import lax
from jax.experimental import pallas as pl
from jax.experimental.pallas import tpu as pltpu
from jax.sharding import PartitionSpec as P

EPSILON = 1e-06
NEGATIVE_FLOOR = -1e30


def padded_2(block, sides, width):
    for axis, dim in sides:
        count = lax.axis_size(axis)
        forward = [(i, i + 1) for i in range(count - 1)]
        backward = [(target, source) for source, target in forward]
        low = lax.ppermute(
            lax.slice_in_dim(block, block.shape[dim] - width, None, axis=dim), axis, forward
        )
        high = lax.ppermute(lax.slice_in_dim(block, 0, width, axis=dim), axis, backward)
        block = jnp.concatenate([low, block, high], axis=dim)
    return block


def normalize(values, gain_table):
    token_count = values.shape[0]
    head_count, head_size = gain_table.shape
    split = values.astype(jnp.float32).reshape(token_count, head_count, head_size)
    mean_square = jnp.mean(split * split, axis=-1, keepdims=True)
    return (split * lax.rsqrt(mean_square + EPSILON) * gain_table).astype(jnp.bfloat16)


def layer_terms(queries, key_rows, value_rows, score_scale):
    scores = (
        jnp.einsum("qhd,khd->hqk", queries, key_rows, preferred_element_type=jnp.float32)
        * score_scale
    )
    layer_max = jnp.max(scores, axis=-1)
    unnormed = jnp.exp(scores - layer_max[..., None]).astype(jnp.bfloat16)
    layer_sum = jnp.sum(unnormed.astype(jnp.float32), axis=-1)
    weighted = jnp.einsum("hqk,khd->qhd", unnormed, value_rows, preferred_element_type=jnp.float32)
    return (layer_max, layer_sum, weighted)


def combine(maxima, layer_sums, weighted, presence):
    mask = presence[:, None, None]
    maxima = jnp.where(mask, maxima, NEGATIVE_FLOOR)
    layer_sums = jnp.where(mask, layer_sums, 0.0)
    overall = jnp.max(maxima, axis=0)
    factors = jnp.exp(maxima - overall)
    denominator = jnp.sum(factors * layer_sums, axis=0)
    numerator = jnp.sum(jnp.transpose(factors, (0, 2, 1))[..., None] * weighted, axis=0)
    return numerator / jnp.transpose(denominator)[..., None]


def body(stream, query_input, key_input, value_input, q_gain, k_gain, out_weight, gate):
    token_count, feature_count = query_input.shape
    head_count, head_size = q_gain.shape
    score_scale = 1.0 / math.sqrt(head_size)
    queries = normalize(query_input, q_gain)
    normed_keys = normalize(key_input, k_gain).reshape(token_count, feature_count)
    layered = jnp.stack([normed_keys, value_input], axis=0)[None, None]
    padded = padded_2(layered, (("seq", 0), ("row", 1)), 1)
    padded = padded.reshape(9, 2, token_count, feature_count)
    key_stack = padded[:, 0].reshape(9, token_count, head_count, head_size)
    value_stack = padded[:, 1].reshape(9, token_count, head_count, head_size)
    time_index = lax.axis_index("seq")
    time_count = lax.axis_size("seq")
    height_index = lax.axis_index("row")
    height_count = lax.axis_size("row")
    time_present = [time_index > 0, time_index >= 0, time_index < time_count - 1]
    height_present = [height_index > 0, height_index >= 0, height_index < height_count - 1]
    presence = jnp.stack(
        [time_flag & height_flag for time_flag in time_present for height_flag in height_present]
    )
    result_set = [
        layer_terms(queries, key_stack[layer_index], value_stack[layer_index], score_scale)
        for layer_index in range(9)
    ]
    maxima = jnp.stack([entry[0] for entry in result_set])
    layer_sums = jnp.stack([entry[1] for entry in result_set])
    weighted = jnp.stack([entry[2] for entry in result_set])
    attention = (
        combine(maxima, layer_sums, weighted, presence)
        .reshape(token_count, feature_count)
        .astype(jnp.bfloat16)
    )
    all_heads = lax.all_gather(attention, "col", axis=1, tiled=True)
    projected = jnp.dot(
        all_heads,
        lax.all_gather(out_weight, "row", axis=0, tiled=True),
        preferred_element_type=jnp.float32,
    )
    return (stream.astype(jnp.float32) + gate * projected).astype(jnp.bfloat16)


ABSENT = 1e30
LOG2_E = 1.4426950408889634
MIB = 1 << 20
CHUNKS = 2
FIRST_VMEM = 60 * MIB
LAST_VMEM = 16 * MIB


def vmem_spec():
    return pl.BlockSpec(memory_space=pltpu.VMEM)


def hbm_spec():
    return pl.BlockSpec(memory_space=pltpu.HBM)


def prep_kernel(
    q_hbm, k_hbm, v_hbm, qg_hbm, kg_hbm, w_hbm, kv_send, kvw_keep, q_send, q_keep, *rest
):
    q_ref, k_ref, v_ref, qg_ref, kg_ref, sems = rest
    mine = lax.axis_index("seq")
    half = q_keep.shape[1]
    head_size = qg_ref.shape[1]
    count = half // head_size
    rows = pl.ds(pl.multiple_of(mine * half, half), half)
    moved = [(kg_hbm, kg_ref), (k_hbm, k_ref), (v_hbm, v_ref), (qg_hbm, qg_ref), (q_hbm, q_ref)]
    for index in range(2):
        moved.append((w_hbm.at[rows, index * half : (index + 1) * half], kvw_keep.at[2 + index]))
    copies = [
        pltpu.make_async_copy(source, target, sems.at[index]) for index, (source, target) in enumerate(moved)
    ]
    for copy in copies:
        copy.start()

    def normed(ref, gain_ref, part, out):
        for index in range(count):
            start = pl.multiple_of(part * half + index * head_size, head_size)
            x = ref[:, pl.ds(start, head_size)].astype(jnp.float32)
            mean_square = jnp.mean(x * x, axis=-1, keepdims=True)
            gain = gain_ref[pl.ds(part * count + index, 1), :]
            scaled = x * lax.rsqrt(mean_square + EPSILON) * gain
            out[:, index * head_size : (index + 1) * head_size] = scaled.astype(jnp.bfloat16)

    halves = ((1 - mine, kv_send, q_send), (mine, kvw_keep, q_keep))
    copies[0].wait()
    copies[1].wait()
    for part, kv_out, _ in halves:
        normed(k_ref, kg_ref, part, kv_out.at[0])
    copies[2].wait()
    for part, kv_out, _ in halves:
        kv_out[1] = v_ref[:, pl.ds(pl.multiple_of(part * half, half), half)]
    copies[3].wait()
    copies[4].wait()
    for part, _, q_out in halves:
        normed(q_ref, qg_ref, part, q_out)
    for copy in copies[5:]:
        copy.wait()


def prep(q, k, v, q_gain, k_gain, out_weight):
    rows, width = q.shape
    half = width // 2
    one = jax.ShapeDtypeStruct((rows, half), jnp.bfloat16)
    two = jax.ShapeDtypeStruct((2, rows, half), jnp.bfloat16)
    four = jax.ShapeDtypeStruct((4, rows, half), jnp.bfloat16)
    block = pltpu.VMEM((rows, width), jnp.bfloat16)
    gain = pltpu.VMEM(q_gain.shape, jnp.float32)
    return pl.pallas_call(
        prep_kernel,
        out_shape=[two, four, one, one],
        in_specs=[hbm_spec()] * 6,
        out_specs=[vmem_spec()] * 4,
        scratch_shapes=[block, block, block, gain, gain, pltpu.SemaphoreType.DMA((7,))],
        compiler_params=pltpu.CompilerParams(vmem_limit_bytes=FIRST_VMEM),
        cost_estimate=pl.CostEstimate(flops=rows * width * 16, bytes_accessed=rows * width * 12, transcendentals=0),
    )(q, k, v, q_gain, k_gain, out_weight)


def attend_kernel(scale, first, head_size, times, *refs):
    queries, refs = refs[: len(times)], refs[len(times) :]
    kv0, kv1, kv2 = refs[:3]
    refs = refs[3:]
    height = lax.axis_index("row")
    flags = [None, None, (height > 0) & (height < lax.axis_size("row") - 1)]
    rows = kv0.shape[1]
    factor = scale * LOG2_E
    ones = jnp.ones((rows, head_size), jnp.bfloat16)

    def head(index, unused):
        columns = pl.ds(pl.multiple_of(index * head_size, head_size), head_size)
        keys = [kv[0, :, columns] for kv in (kv0, kv1, kv2)]
        values = [jnp.concatenate([kv[1, :, columns], ones], axis=1) for kv in (kv0, kv1, kv2)]
        for which, q_ref in zip(times, queries):
            q = q_ref[:, columns]
            scores = [
                lax.dot_general(q, key, (((1,), (1,)), ((), ())), preferred_element_type=jnp.float32)
                for key in keys
            ]
            top = None
            for flag, score in zip(flags, scores):
                part = score[:, :head_size]
                for start in range(head_size, rows, head_size):
                    part = jnp.maximum(part, score[:, start : start + head_size])
                if flag is not None:
                    part = jnp.where(flag, part, NEGATIVE_FLOOR)
                top = part if top is None else jnp.maximum(top, part)
            top = jnp.max(top, axis=1, keepdims=True)
            total = None
            if not first:
                m_in, acc_in = refs[:2]
                before = m_in[index, which][:, :1]
                top = jnp.maximum(before, top)
                total = acc_in[index, which] * jnp.exp2((before - top) * factor)
            for flag, score, value in zip(flags, scores, values):
                shift = top if flag is None else jnp.where(flag, top, ABSENT)
                weights = jnp.exp2((score - shift) * factor).astype(jnp.bfloat16)
                term = jnp.dot(weights, value, preferred_element_type=jnp.float32)
                total = term if total is None else total + term
            if first:
                m_out, acc_out = refs
                m_out[index, which] = jnp.broadcast_to(top, (rows, head_size))
                acc_out[index, which] = total
            else:
                out = refs[2]
                out[:, columns] = (total[:, :head_size] / total[:, head_size:]).astype(jnp.bfloat16)
        return unused

    lax.fori_loop(0, queries[0].shape[1] // head_size, head, 0)


def attend(times, queries, layers, head_size, carry=None):
    rows, width = queries[0].shape
    heads = width // head_size
    vmem = pl.BlockSpec(memory_space=pltpu.VMEM)
    arguments = [*queries, *layers]
    if carry is None:
        out_shape = [
            jax.ShapeDtypeStruct((heads, 2, rows, head_size), jnp.float32),
            jax.ShapeDtypeStruct((heads, 2, rows, 2 * head_size), jnp.float32),
        ]
        out_specs = [vmem, vmem]
    else:
        arguments += list(carry)
        out_shape = jax.ShapeDtypeStruct((rows, width), jnp.bfloat16)
        out_specs = vmem
    return pl.pallas_call(
        functools.partial(attend_kernel, 1.0 / math.sqrt(head_size), carry is None, head_size, times),
        out_shape=out_shape,
        in_specs=[vmem] * len(arguments),
        out_specs=out_specs,
        compiler_params=pltpu.CompilerParams(vmem_limit_bytes=16 * MIB),
        cost_estimate=pl.CostEstimate(
            flops=heads * len(times) * rows * 3 * rows * head_size * 8,
            bytes_accessed=8 * MIB,
            transcendentals=heads * len(times) * rows * 3 * rows,
        ),
    )(*arguments)


def plane_sum(pieces, weights, spans, write):
    shift = lax.axis_index("row") ^ lax.axis_index("col")
    for case in range(4):

        @pl.when(shift == case)
        def _(case=case):
            for part, (low, high) in enumerate(spans):
                total = None
                for index, piece in enumerate(pieces):
                    term = jnp.dot(piece, weights(index ^ case, part, low, high), preferred_element_type=jnp.float32)
                    total = term if total is None else total + term
                write(part, low, high, total)


def weight_of(kvw, kvw_pair, kvw_mid, second, third, which, part):
    if which == 2:
        return second[part][0][...] + second[part][1][...]
    if which == 3:
        return kvw_mid[2 + part] + third[part][...]
    return (kvw, kvw_pair)[which][2 + part]


def peer_kernel(part, a0, a1, a2, a3, kvw, kvw_pair, kvw_mid, s0, s1, t0, out):
    def write(unused, low, high, total):
        out[...] = total.astype(out.dtype)

    def weights(which, unused, low, high):
        return weight_of(kvw, kvw_pair, kvw_mid, {part: (s0, s1)}, {part: t0}, which, part)

    plane_sum([a[...] for a in (a0, a1, a2, a3)], weights, [(0, out.shape[1])], write)


def own_kernel(spans, a0, a1, a2, a3, kvw, kvw_pair, kvw_mid, gate, stream_hbm, *rest):
    second, third = (rest[0:2], rest[3:5]), (rest[2], rest[5])
    out, stream, sem = rest[6:]
    copy = pltpu.make_async_copy(stream_hbm, stream, sem)
    copy.start()
    copy.wait()

    def write(part, low, high, total):
        out[:, low:high] = stream[:, low:high].astype(jnp.float32) + gate[:, low:high] * total

    def weights(which, part, low, high):
        return weight_of(kvw, kvw_pair, kvw_mid, second, third, which, part)

    plane_sum([a[...] for a in (a0, a1, a2, a3)], weights, spans, write)


def final_kernel(spans, base, gate, *rest):
    received, out_hbm, out, sems = rest[:-3], rest[-3], rest[-2], rest[-1]
    copies = []
    for part, (low, high) in enumerate(spans):
        total = base[:, low:high] + gate[:, low:high] * received[part][...].astype(jnp.float32)
        out[:, low:high] = total.astype(out.dtype)
        copies.append(pltpu.make_async_copy(out.at[:, low:high], out_hbm.at[:, low:high], sems.at[part]))
        copies[-1].start()
    for copy in copies:
        copy.wait()


def pair_body(stream, query_input, key_input, value_input, q_gain, k_gain, out_weight, gate):
    head_size = q_gain.shape[1]
    tokens, width = stream.shape
    rows = lax.axis_size("row")
    spans = [(width * i // CHUNKS, width * (i + 1) // CHUNKS) for i in range(CHUNKS)]

    def swap(x):
        return lax.ppermute(x, "seq", [(0, 1), (1, 0)])

    def pair(x):
        return lax.ppermute(x, "row", [(i, i ^ 1) for i in range(4)])

    def middle(x):
        return lax.ppermute(x, "row", [(1, 2), (2, 1)])

    def along(x, axis, mask):
        return lax.ppermute(x, axis, [(i, i ^ mask) for i in range(4)])

    def call(kernel, arguments, specs, out_shape, out_spec, scratch, flops):
        return pl.pallas_call(
            kernel,
            out_shape=out_shape,
            in_specs=specs,
            out_specs=out_spec,
            scratch_shapes=scratch,
            compiler_params=pltpu.CompilerParams(vmem_limit_bytes=LAST_VMEM),
            cost_estimate=pl.CostEstimate(flops=flops, bytes_accessed=2 * MIB, transcendentals=0),
        )(*arguments)

    def inward(x):
        return lax.ppermute(x, "row", [(1, 0), (2, 3)])

    barrier = lax.optimization_barrier
    kv_send, kvw, q_send, q_keep = prep(query_input, key_input, value_input, q_gain, k_gain, out_weight)
    kv_peer = swap(kv_send)
    kvw_pair, kvw_mid = pair(kvw), middle(kvw)
    q_peer = swap(q_send)
    peer_pair, peer_mid = pair(kv_peer), middle(kv_peer)

    carry = attend((0, 1), [q_keep, q_peer], [kvw, kvw_pair, kvw_mid], head_size)
    first_pair, first_mid, carry = barrier((kvw_pair[2], kvw_mid[2], carry))
    forward = [middle(first_pair)]
    second = [inward(first_mid)]
    layers = [kv_peer, peer_pair, peer_mid]
    theirs = attend((1,), [q_peer], layers, head_size, carry)
    theirs, forward[0] = barrier((theirs, forward[0]))
    across_theirs, beside_theirs = along(theirs, "col", 2), along(theirs, "col", 1)
    third = [inward(forward[0])]
    next_pair, next_mid, carry = barrier((kvw_pair[3], kvw_mid[3], carry, theirs))[:3]
    forward.append(middle(next_pair))
    second.append(inward(next_mid))
    third.append(inward(forward[1]))
    mine = attend((0,), [q_keep], layers, head_size, carry)
    across_mine, beside_mine = along(mine, "col", 2), along(mine, "col", 1)
    weights = [[forward[part], second[part], third[part]] for part in range(2)]

    gate = gate.reshape(1, width)
    vmem, hbm = vmem_spec(), hbm_spec()
    groups = [theirs, beside_theirs, across_theirs, along(across_theirs, "col", 1)]
    received = []
    for part, (low, high) in enumerate(spans):
        sent = call(
            functools.partial(peer_kernel, part),
            [*groups, kvw, kvw_pair, kvw_mid, *weights[part]],
            [vmem] * 10,
            jax.ShapeDtypeStruct((tokens, high - low), jnp.bfloat16),
            vmem,
            [],
            tokens * width * (high - low) * 4,
        )
        if part == 0:
            sent, groups[0] = barrier((sent, groups[0]))
        received.append(swap(sent))
    groups = [mine, beside_mine, across_mine, along(across_mine, "col", 1)]
    base = call(
        functools.partial(own_kernel, spans),
        [*groups, kvw, kvw_pair, kvw_mid, gate, stream, *weights[0], *weights[1]],
        [vmem] * 8 + [hbm] + [vmem] * 6,
        jax.ShapeDtypeStruct((tokens, width), jnp.float32),
        vmem,
        [pltpu.VMEM((tokens, width), stream.dtype), pltpu.SemaphoreType.DMA(())],
        tokens * width * width * 4,
    )
    return call(
        functools.partial(final_kernel, spans),
        [base, gate, *received],
        [vmem] * (2 + CHUNKS),
        jax.ShapeDtypeStruct((tokens, width), jnp.bfloat16),
        hbm,
        [pltpu.VMEM((tokens, width), jnp.bfloat16), pltpu.SemaphoreType.DMA((CHUNKS,))],
        tokens * width * 4,
    )


def solution(mesh):
    placed = (
        P(("seq", "row"), "col"),
        P(("seq", "row"), "col"),
        P(("seq", "row"), "col"),
        P(("seq", "row"), "col"),
        P("col", None),
        P("col", None),
        P("row", "col"),
        P("col"),
    )
    shape = mesh.shape
    paired = shape["seq"] == 2 and shape["row"] == 4 and shape["col"] == 4
    return jax.shard_map(
        pair_body if paired else body, mesh=mesh, in_specs=placed, out_specs=P(("seq", "row"), "col"), check_vma=False
    )
```

```python
import functools
import math

import jax
import jax.numpy as jnp
from jax import lax
from jax.experimental import pallas as pl
from jax.experimental.pallas import tpu as pltpu
from jax.sharding import PartitionSpec as P

EPSILON = 1e-06
NEGATIVE_FLOOR = -1e30


def padded_2(block, sides, width):
    for axis, dim in sides:
        count = lax.axis_size(axis)
        forward = [(i, i + 1) for i in range(count - 1)]
        backward = [(target, source) for source, target in forward]
        low = lax.ppermute(
            lax.slice_in_dim(block, block.shape[dim] - width, None, axis=dim), axis, forward
        )
        high = lax.ppermute(lax.slice_in_dim(block, 0, width, axis=dim), axis, backward)
        block = jnp.concatenate([low, block, high], axis=dim)
    return block


def normalize(values, gain_table):
    token_count = values.shape[0]
    head_count, head_size = gain_table.shape
    split = values.astype(jnp.float32).reshape(token_count, head_count, head_size)
    mean_square = jnp.mean(split * split, axis=-1, keepdims=True)
    return (split * lax.rsqrt(mean_square + EPSILON) * gain_table).astype(jnp.bfloat16)


def layer_terms(queries, key_rows, value_rows, score_scale):
    scores = (
        jnp.einsum("qhd,khd->hqk", queries, key_rows, preferred_element_type=jnp.float32)
        * score_scale
    )
    layer_max = jnp.max(scores, axis=-1)
    unnormed = jnp.exp(scores - layer_max[..., None]).astype(jnp.bfloat16)
    layer_sum = jnp.sum(unnormed.astype(jnp.float32), axis=-1)
    weighted = jnp.einsum("hqk,khd->qhd", unnormed, value_rows, preferred_element_type=jnp.float32)
    return (layer_max, layer_sum, weighted)


def combine(maxima, layer_sums, weighted, presence):
    mask = presence[:, None, None]
    maxima = jnp.where(mask, maxima, NEGATIVE_FLOOR)
    layer_sums = jnp.where(mask, layer_sums, 0.0)
    overall = jnp.max(maxima, axis=0)
    factors = jnp.exp(maxima - overall)
    denominator = jnp.sum(factors * layer_sums, axis=0)
    numerator = jnp.sum(jnp.transpose(factors, (0, 2, 1))[..., None] * weighted, axis=0)
    return numerator / jnp.transpose(denominator)[..., None]


def body(stream, query_input, key_input, value_input, q_gain, k_gain, out_weight, gate):
    token_count, feature_count = query_input.shape
    head_count, head_size = q_gain.shape
    score_scale = 1.0 / math.sqrt(head_size)
    queries = normalize(query_input, q_gain)
    normed_keys = normalize(key_input, k_gain).reshape(token_count, feature_count)
    layered = jnp.stack([normed_keys, value_input], axis=0)[None, None]
    padded = padded_2(layered, (("seq", 0), ("row", 1)), 1)
    padded = padded.reshape(9, 2, token_count, feature_count)
    key_stack = padded[:, 0].reshape(9, token_count, head_count, head_size)
    value_stack = padded[:, 1].reshape(9, token_count, head_count, head_size)
    time_index = lax.axis_index("seq")
    time_count = lax.axis_size("seq")
    height_index = lax.axis_index("row")
    height_count = lax.axis_size("row")
    time_present = [time_index > 0, time_index >= 0, time_index < time_count - 1]
    height_present = [height_index > 0, height_index >= 0, height_index < height_count - 1]
    presence = jnp.stack(
        [time_flag & height_flag for time_flag in time_present for height_flag in height_present]
    )
    result_set = [
        layer_terms(queries, key_stack[layer_index], value_stack[layer_index], score_scale)
        for layer_index in range(9)
    ]
    maxima = jnp.stack([entry[0] for entry in result_set])
    layer_sums = jnp.stack([entry[1] for entry in result_set])
    weighted = jnp.stack([entry[2] for entry in result_set])
    attention = (
        combine(maxima, layer_sums, weighted, presence)
        .reshape(token_count, feature_count)
        .astype(jnp.bfloat16)
    )
    all_heads = lax.all_gather(attention, "col", axis=1, tiled=True)
    projected = jnp.dot(
        all_heads,
        lax.all_gather(out_weight, "row", axis=0, tiled=True),
        preferred_element_type=jnp.float32,
    )
    return (stream.astype(jnp.float32) + gate * projected).astype(jnp.bfloat16)


ABSENT = 1e30
LOG2_E = 1.4426950408889634
MIB = 1 << 20
CHUNKS = 2
FIRST_VMEM = 60 * MIB
LAST_VMEM = 16 * MIB


def vmem_spec():
    return pl.BlockSpec(memory_space=pltpu.VMEM)


def hbm_spec():
    return pl.BlockSpec(memory_space=pltpu.HBM)


def prep_kernel(
    q_hbm, k_hbm, v_hbm, qg_hbm, kg_hbm, w_hbm, kv_send, kvw_keep, q_send, q_keep, *rest
):
    q_ref, k_ref, qg_ref, kg_ref, sems = rest
    mine = lax.axis_index("seq")
    half = q_keep.shape[1]
    head_size = qg_ref.shape[1]
    count = half // head_size
    rows = pl.ds(pl.multiple_of(mine * half, half), half)
    moved = [(kg_hbm, kg_ref), (k_hbm, k_ref), (qg_hbm, qg_ref), (q_hbm, q_ref)]
    for part, out in ((1 - mine, kv_send), (mine, kvw_keep)):
        moved.append((v_hbm.at[:, pl.ds(pl.multiple_of(part * half, half), half)], out.at[1]))
    for index in range(2):
        moved.append((w_hbm.at[rows, index * half : (index + 1) * half], kvw_keep.at[2 + index]))
    copies = [
        pltpu.make_async_copy(source, target, sems.at[index]) for index, (source, target) in enumerate(moved)
    ]
    for copy in copies:
        copy.start()

    def normed(ref, gain_ref, part, out):
        for index in range(count):
            start = pl.multiple_of(part * half + index * head_size, head_size)
            x = ref[:, pl.ds(start, head_size)].astype(jnp.float32)
            mean_square = jnp.mean(x * x, axis=-1, keepdims=True)
            gain = gain_ref[pl.ds(part * count + index, 1), :]
            scaled = x * lax.rsqrt(mean_square + EPSILON) * gain
            out[:, index * head_size : (index + 1) * head_size] = scaled.astype(jnp.bfloat16)

    halves = ((1 - mine, kv_send, q_send), (mine, kvw_keep, q_keep))
    copies[0].wait()
    copies[1].wait()
    for part, kv_out, _ in halves:
        normed(k_ref, kg_ref, part, kv_out.at[0])
    copies[2].wait()
    copies[3].wait()
    for part, _, q_out in halves:
        normed(q_ref, qg_ref, part, q_out)
    for copy in copies[4:]:
        copy.wait()


def prep(q, k, v, q_gain, k_gain, out_weight):
    rows, width = q.shape
    half = width // 2
    one = jax.ShapeDtypeStruct((rows, half), jnp.bfloat16)
    two = jax.ShapeDtypeStruct((2, rows, half), jnp.bfloat16)
    four = jax.ShapeDtypeStruct((4, rows, half), jnp.bfloat16)
    block = pltpu.VMEM((rows, width), jnp.bfloat16)
    gain = pltpu.VMEM(q_gain.shape, jnp.float32)
    return pl.pallas_call(
        prep_kernel,
        out_shape=[two, four, one, one],
        in_specs=[hbm_spec()] * 6,
        out_specs=[vmem_spec()] * 4,
        scratch_shapes=[block, block, gain, gain, pltpu.SemaphoreType.DMA((8,))],
        compiler_params=pltpu.CompilerParams(vmem_limit_bytes=FIRST_VMEM),
        cost_estimate=pl.CostEstimate(flops=rows * width * 16, bytes_accessed=rows * width * 12, transcendentals=0),
    )(q, k, v, q_gain, k_gain, out_weight)


def attend_kernel(scale, first, head_size, times, *refs):
    queries, refs = refs[: len(times)], refs[len(times) :]
    kv0, kv1, kv2 = refs[:3]
    refs = refs[3:]
    height = lax.axis_index("row")
    flags = [None, None, (height > 0) & (height < lax.axis_size("row") - 1)]
    rows = kv0.shape[1]
    factor = scale * LOG2_E
    ones = jnp.ones((rows, head_size), jnp.bfloat16)

    for index in range(queries[0].shape[1] // head_size):
        columns = slice(index * head_size, (index + 1) * head_size)
        keys = [kv[0, :, columns] for kv in (kv0, kv1, kv2)]
        values = [jnp.concatenate([kv[1, :, columns], ones], axis=1) for kv in (kv0, kv1, kv2)]
        for which, q_ref in zip(times, queries):
            q = q_ref[:, columns]
            scores = [
                lax.dot_general(q, key, (((1,), (1,)), ((), ())), preferred_element_type=jnp.float32)
                for key in keys
            ]
            top = None
            for flag, score in zip(flags, scores):
                part = score[:, :head_size]
                for start in range(head_size, rows, head_size):
                    part = jnp.maximum(part, score[:, start : start + head_size])
                if flag is not None:
                    part = jnp.where(flag, part, NEGATIVE_FLOOR)
                top = part if top is None else jnp.maximum(top, part)
            top = jnp.max(top, axis=1, keepdims=True)
            total = None
            if not first:
                m_in, acc_in = refs[:2]
                before = m_in[index, which][:, :1]
                top = jnp.maximum(before, top)
                total = acc_in[index, which] * jnp.exp2((before - top) * factor)
            for flag, score, value in zip(flags, scores, values):
                shift = top if flag is None else jnp.where(flag, top, ABSENT)
                weights = jnp.exp2((score - shift) * factor).astype(jnp.bfloat16)
                term = jnp.dot(weights, value, preferred_element_type=jnp.float32)
                total = term if total is None else total + term
            if first:
                m_out, acc_out = refs
                m_out[index, which] = jnp.broadcast_to(top, (rows, head_size))
                acc_out[index, which] = total
            else:
                out = refs[2]
                out[:, columns] = (total[:, :head_size] / total[:, head_size:]).astype(jnp.bfloat16)


def attend(times, queries, layers, head_size, carry=None):
    rows, width = queries[0].shape
    heads = width // head_size
    vmem = pl.BlockSpec(memory_space=pltpu.VMEM)
    arguments = [*queries, *layers]
    if carry is None:
        out_shape = [
            jax.ShapeDtypeStruct((heads, 2, rows, head_size), jnp.float32),
            jax.ShapeDtypeStruct((heads, 2, rows, 2 * head_size), jnp.float32),
        ]
        out_specs = [vmem, vmem]
    else:
        arguments += list(carry)
        out_shape = jax.ShapeDtypeStruct((rows, width), jnp.bfloat16)
        out_specs = vmem
    return pl.pallas_call(
        functools.partial(attend_kernel, 1.0 / math.sqrt(head_size), carry is None, head_size, times),
        out_shape=out_shape,
        in_specs=[vmem] * len(arguments),
        out_specs=out_specs,
        compiler_params=pltpu.CompilerParams(vmem_limit_bytes=16 * MIB),
        cost_estimate=pl.CostEstimate(
            flops=heads * len(times) * rows * 3 * rows * head_size * 8,
            bytes_accessed=8 * MIB,
            transcendentals=heads * len(times) * rows * 3 * rows,
        ),
    )(*arguments)


def plane_sum(pieces, weights, spans, write):
    shift = lax.axis_index("row") ^ lax.axis_index("col")
    for case in range(4):

        @pl.when(shift == case)
        def _(case=case):
            for part, (low, high) in enumerate(spans):
                total = None
                for index, piece in enumerate(pieces):
                    term = jnp.dot(piece, weights(index ^ case, part, low, high), preferred_element_type=jnp.float32)
                    total = term if total is None else total + term
                write(part, low, high, total)


def weight_of(kvw, kvw_pair, kvw_mid, inner, forward, outer, which, part):
    if which == 2:
        return inner[part] + forward(part)
    if which == 3:
        return kvw_mid[2 + part] + outer[part][...]
    return (kvw, kvw_pair)[which][2 + part]


def peer_kernel(part, a0, a1, a2, a3, kvw, kvw_pair, kvw_mid, inner, forward, outer, out):
    def write(unused, low, high, total):
        out[...] = total.astype(out.dtype)

    def weights(which, unused, low, high):
        return weight_of(kvw, kvw_pair, kvw_mid, inner, lambda p: forward[...], {part: outer}, which, part)

    plane_sum([a[...] for a in (a0, a1, a2, a3)], weights, [(0, out.shape[1])], write)


def own_kernel(spans, a0, a1, a2, a3, kvw, kvw_pair, kvw_mid, inner, gate, stream_hbm, *rest):
    forward, outer = rest[:2], rest[2 : 4]
    out, stream, sem = rest[4 :]
    copy = pltpu.make_async_copy(stream_hbm, stream, sem)
    copy.start()
    copy.wait()

    def write(part, low, high, total):
        out[:, low:high] = stream[:, low:high].astype(jnp.float32) + gate[:, low:high] * total

    def weights(which, part, low, high):
        return weight_of(kvw, kvw_pair, kvw_mid, inner, lambda p: forward[p][...], outer, which, part)

    plane_sum([a[...] for a in (a0, a1, a2, a3)], weights, spans, write)


def final_kernel(spans, base, gate, *rest):
    received, out_hbm, out, sems = rest[:-3], rest[-3], rest[-2], rest[-1]
    copies = []
    for part, (low, high) in enumerate(spans):
        total = base[:, low:high] + gate[:, low:high] * received[part][...].astype(jnp.float32)
        out[:, low:high] = total.astype(out.dtype)
        copies.append(pltpu.make_async_copy(out.at[:, low:high], out_hbm.at[:, low:high], sems.at[part]))
        copies[-1].start()
    for copy in copies:
        copy.wait()


def pair_body(stream, query_input, key_input, value_input, q_gain, k_gain, out_weight, gate):
    head_size = q_gain.shape[1]
    tokens, width = stream.shape
    rows = lax.axis_size("row")
    spans = [(width * i // CHUNKS, width * (i + 1) // CHUNKS) for i in range(CHUNKS)]

    def swap(x):
        return lax.ppermute(x, "seq", [(0, 1), (1, 0)])

    def pair(x):
        return lax.ppermute(x, "row", [(i, i ^ 1) for i in range(4)])

    def middle(x):
        return lax.ppermute(x, "row", [(1, 2), (2, 1)])

    def along(x, axis, mask):
        return lax.ppermute(x, axis, [(i, i ^ mask) for i in range(4)])

    def call(kernel, arguments, specs, out_shape, out_spec, scratch, flops):
        return pl.pallas_call(
            kernel,
            out_shape=out_shape,
            in_specs=specs,
            out_specs=out_spec,
            scratch_shapes=scratch,
            compiler_params=pltpu.CompilerParams(vmem_limit_bytes=LAST_VMEM),
            cost_estimate=pl.CostEstimate(flops=flops, bytes_accessed=2 * MIB, transcendentals=0),
        )(*arguments)

    def inward(x):
        return lax.ppermute(x, "row", [(1, 0), (2, 3)])

    barrier = lax.optimization_barrier
    kv_send, kvw, q_send, q_keep = prep(query_input, key_input, value_input, q_gain, k_gain, out_weight)
    kv_peer = swap(kv_send)
    kvw_pair, kvw_mid = pair(kvw), middle(kvw)
    q_peer = swap(q_send)
    peer_pair, peer_mid = pair(kv_peer), middle(kv_peer)

    carry = attend((0, 1), [q_keep, q_peer], [kvw, kvw_pair, kvw_mid], head_size)
    first_pair, early_mid, carry = barrier((kvw_pair[2], kvw_mid[2:], carry))
    inner, forwards = inward(early_mid), [middle(first_pair)]
    layers = [kv_peer, peer_pair, peer_mid]
    theirs = attend((1,), [q_peer], layers, head_size, carry)
    theirs, forwards[0] = barrier((theirs, forwards[0]))
    across_theirs, beside_theirs = along(theirs, "col", 2), along(theirs, "col", 1)
    next_pair = barrier((kvw_pair[3], theirs))[0]
    forwards.append(middle(next_pair))
    outer = [inward(forwards[part]) for part in range(2)]

    gate = gate.reshape(1, width)
    vmem, hbm = vmem_spec(), hbm_spec()
    groups = [theirs, beside_theirs, across_theirs, along(across_theirs, "col", 1)]
    sents = []
    for part, (low, high) in enumerate(spans):
        sent = call(
            functools.partial(peer_kernel, part),
            [*groups, kvw, kvw_pair, kvw_mid, inner, forwards[part], outer[part]],
            [vmem] * 10,
            jax.ShapeDtypeStruct((tokens, high - low), jnp.bfloat16),
            vmem,
            [],
            tokens * width * (high - low) * 4,
        )
        if part == 0:
            sent, groups[0] = barrier((sent, groups[0]))
        sents.append(sent)
    received = [swap(sent) for sent in sents]
    carry, forwards[1] = barrier((carry, forwards[1]))
    mine = attend((0,), [q_keep], layers, head_size, carry)
    across_mine, beside_mine = along(mine, "col", 2), along(mine, "col", 1)
    groups = [mine, beside_mine, across_mine, along(across_mine, "col", 1)]
    base = call(
        functools.partial(own_kernel, spans),
        [*groups, kvw, kvw_pair, kvw_mid, inner, gate, stream, *forwards, *outer],
        [vmem] * 9 + [hbm] + [vmem] * 4,
        jax.ShapeDtypeStruct((tokens, width), jnp.float32),
        vmem,
        [pltpu.VMEM((tokens, width), stream.dtype), pltpu.SemaphoreType.DMA(())],
        tokens * width * width * 4,
    )
    return call(
        functools.partial(final_kernel, spans),
        [base, gate, *received],
        [vmem] * (2 + CHUNKS),
        jax.ShapeDtypeStruct((tokens, width), jnp.bfloat16),
        hbm,
        [pltpu.VMEM((tokens, width), jnp.bfloat16), pltpu.SemaphoreType.DMA((CHUNKS,))],
        tokens * width * 4,
    )


def solution(mesh):
    placed = (
        P(("seq", "row"), "col"),
        P(("seq", "row"), "col"),
        P(("seq", "row"), "col"),
        P(("seq", "row"), "col"),
        P("col", None),
        P("col", None),
        P("row", "col"),
        P("col"),
    )
    shape = mesh.shape
    paired = shape["seq"] == 2 and shape["row"] == 4 and shape["col"] == 4
    return jax.shard_map(
        pair_body if paired else body, mesh=mesh, in_specs=placed, out_specs=P(("seq", "row"), "col"), check_vma=False
    )
```

```python
import functools
import math

import jax
import jax.numpy as jnp
from jax import lax
from jax.experimental import pallas as pl
from jax.experimental.pallas import tpu as pltpu
from jax.sharding import PartitionSpec as P

EPSILON = 1e-06
NEGATIVE_FLOOR = -1e30


def padded_2(block, sides, width):
    for axis, dim in sides:
        count = lax.axis_size(axis)
        forward = [(i, i + 1) for i in range(count - 1)]
        backward = [(target, source) for source, target in forward]
        low = lax.ppermute(
            lax.slice_in_dim(block, block.shape[dim] - width, None, axis=dim), axis, forward
        )
        high = lax.ppermute(lax.slice_in_dim(block, 0, width, axis=dim), axis, backward)
        block = jnp.concatenate([low, block, high], axis=dim)
    return block


def normalize(values, gain_table):
    token_count = values.shape[0]
    head_count, head_size = gain_table.shape
    split = values.astype(jnp.float32).reshape(token_count, head_count, head_size)
    mean_square = jnp.mean(split * split, axis=-1, keepdims=True)
    return (split * lax.rsqrt(mean_square + EPSILON) * gain_table).astype(jnp.bfloat16)


def layer_terms(queries, key_rows, value_rows, score_scale):
    scores = (
        jnp.einsum("qhd,khd->hqk", queries, key_rows, preferred_element_type=jnp.float32)
        * score_scale
    )
    layer_max = jnp.max(scores, axis=-1)
    unnormed = jnp.exp(scores - layer_max[..., None]).astype(jnp.bfloat16)
    layer_sum = jnp.sum(unnormed.astype(jnp.float32), axis=-1)
    weighted = jnp.einsum("hqk,khd->qhd", unnormed, value_rows, preferred_element_type=jnp.float32)
    return (layer_max, layer_sum, weighted)


def combine(maxima, layer_sums, weighted, presence):
    mask = presence[:, None, None]
    maxima = jnp.where(mask, maxima, NEGATIVE_FLOOR)
    layer_sums = jnp.where(mask, layer_sums, 0.0)
    overall = jnp.max(maxima, axis=0)
    factors = jnp.exp(maxima - overall)
    denominator = jnp.sum(factors * layer_sums, axis=0)
    numerator = jnp.sum(jnp.transpose(factors, (0, 2, 1))[..., None] * weighted, axis=0)
    return numerator / jnp.transpose(denominator)[..., None]


def body(stream, query_input, key_input, value_input, q_gain, k_gain, out_weight, gate):
    token_count, feature_count = query_input.shape
    head_count, head_size = q_gain.shape
    score_scale = 1.0 / math.sqrt(head_size)
    queries = normalize(query_input, q_gain)
    normed_keys = normalize(key_input, k_gain).reshape(token_count, feature_count)
    layered = jnp.stack([normed_keys, value_input], axis=0)[None, None]
    padded = padded_2(layered, (("seq", 0), ("row", 1)), 1)
    padded = padded.reshape(9, 2, token_count, feature_count)
    key_stack = padded[:, 0].reshape(9, token_count, head_count, head_size)
    value_stack = padded[:, 1].reshape(9, token_count, head_count, head_size)
    time_index = lax.axis_index("seq")
    time_count = lax.axis_size("seq")
    height_index = lax.axis_index("row")
    height_count = lax.axis_size("row")
    time_present = [time_index > 0, time_index >= 0, time_index < time_count - 1]
    height_present = [height_index > 0, height_index >= 0, height_index < height_count - 1]
    presence = jnp.stack(
        [time_flag & height_flag for time_flag in time_present for height_flag in height_present]
    )
    result_set = [
        layer_terms(queries, key_stack[layer_index], value_stack[layer_index], score_scale)
        for layer_index in range(9)
    ]
    maxima = jnp.stack([entry[0] for entry in result_set])
    layer_sums = jnp.stack([entry[1] for entry in result_set])
    weighted = jnp.stack([entry[2] for entry in result_set])
    attention = (
        combine(maxima, layer_sums, weighted, presence)
        .reshape(token_count, feature_count)
        .astype(jnp.bfloat16)
    )
    all_heads = lax.all_gather(attention, "col", axis=1, tiled=True)
    projected = jnp.dot(
        all_heads,
        lax.all_gather(out_weight, "row", axis=0, tiled=True),
        preferred_element_type=jnp.float32,
    )
    return (stream.astype(jnp.float32) + gate * projected).astype(jnp.bfloat16)


ABSENT = 1e30
LOG2_E = 1.4426950408889634
MIB = 1 << 20
CHUNKS = 2
FIRST_VMEM = 60 * MIB
LAST_VMEM = 16 * MIB


def vmem_spec():
    return pl.BlockSpec(memory_space=pltpu.VMEM)


def hbm_spec():
    return pl.BlockSpec(memory_space=pltpu.HBM)


def prep_kernel(
    q_hbm, k_hbm, v_hbm, qg_hbm, kg_hbm, w_hbm, kv_send, kvw_keep, q_send, q_keep, *rest
):
    q_ref, k_ref, qg_ref, kg_ref, sems = rest
    mine = lax.axis_index("seq")
    half = q_keep.shape[1]
    head_size = qg_ref.shape[1]
    count = half // head_size
    rows = pl.ds(pl.multiple_of(mine * half, half), half)
    moved = [(kg_hbm, kg_ref), (k_hbm, k_ref), (qg_hbm, qg_ref), (q_hbm, q_ref)]
    for part, out in ((1 - mine, kv_send), (mine, kvw_keep)):
        moved.append((v_hbm.at[:, pl.ds(pl.multiple_of(part * half, half), half)], out.at[1]))
    for index in range(2):
        moved.append((w_hbm.at[rows, index * half : (index + 1) * half], kvw_keep.at[2 + index]))
    copies = [
        pltpu.make_async_copy(source, target, sems.at[index]) for index, (source, target) in enumerate(moved)
    ]
    for copy in copies:
        copy.start()

    def normed(ref, gain_ref, part, out):
        for index in range(count):
            start = pl.multiple_of(part * half + index * head_size, head_size)
            x = ref[:, pl.ds(start, head_size)].astype(jnp.float32)
            mean_square = jnp.mean(x * x, axis=-1, keepdims=True)
            gain = gain_ref[pl.ds(part * count + index, 1), :]
            scaled = x * lax.rsqrt(mean_square + EPSILON) * gain
            out[:, index * head_size : (index + 1) * head_size] = scaled.astype(jnp.bfloat16)

    halves = ((1 - mine, kv_send, q_send), (mine, kvw_keep, q_keep))
    copies[0].wait()
    copies[1].wait()
    for part, kv_out, _ in halves:
        normed(k_ref, kg_ref, part, kv_out.at[0])
    copies[2].wait()
    copies[3].wait()
    for part, _, q_out in halves:
        normed(q_ref, qg_ref, part, q_out)
    for copy in copies[4:]:
        copy.wait()


def prep(q, k, v, q_gain, k_gain, out_weight):
    rows, width = q.shape
    half = width // 2
    one = jax.ShapeDtypeStruct((rows, half), jnp.bfloat16)
    two = jax.ShapeDtypeStruct((2, rows, half), jnp.bfloat16)
    four = jax.ShapeDtypeStruct((4, rows, half), jnp.bfloat16)
    block = pltpu.VMEM((rows, width), jnp.bfloat16)
    gain = pltpu.VMEM(q_gain.shape, jnp.float32)
    return pl.pallas_call(
        prep_kernel,
        out_shape=[two, four, one, one],
        in_specs=[hbm_spec()] * 6,
        out_specs=[vmem_spec()] * 4,
        scratch_shapes=[block, block, gain, gain, pltpu.SemaphoreType.DMA((8,))],
        compiler_params=pltpu.CompilerParams(vmem_limit_bytes=FIRST_VMEM),
        cost_estimate=pl.CostEstimate(flops=rows * width * 16, bytes_accessed=rows * width * 12, transcendentals=0),
    )(q, k, v, q_gain, k_gain, out_weight)


def attend_kernel(scale, first, head_size, times, *refs):
    queries, refs = refs[: len(times)], refs[len(times) :]
    kv0, kv1, kv2 = refs[:3]
    refs = refs[3:]
    height = lax.axis_index("row")
    flags = [None, None, (height > 0) & (height < lax.axis_size("row") - 1)]
    rows = kv0.shape[1]
    factor = scale * LOG2_E
    ones = jnp.ones((rows, head_size), jnp.bfloat16)

    for index in range(queries[0].shape[1] // head_size):
        columns = slice(index * head_size, (index + 1) * head_size)
        keys = [kv[0, :, columns] for kv in (kv0, kv1, kv2)]
        values = [jnp.concatenate([kv[1, :, columns], ones], axis=1) for kv in (kv0, kv1, kv2)]
        for which, q_ref in zip(times, queries):
            q = q_ref[:, columns]
            scores = [
                lax.dot_general(q, key, (((1,), (1,)), ((), ())), preferred_element_type=jnp.float32)
                for key in keys
            ]
            top = None
            for flag, score in zip(flags, scores):
                part = score[:, :head_size]
                for start in range(head_size, rows, head_size):
                    part = jnp.maximum(part, score[:, start : start + head_size])
                if flag is not None:
                    part = jnp.where(flag, part, NEGATIVE_FLOOR)
                top = part if top is None else jnp.maximum(top, part)
            top = jnp.max(top, axis=1, keepdims=True)
            total = None
            if not first:
                m_in, acc_in = refs[:2]
                before = m_in[index, which][:, :1]
                top = jnp.maximum(before, top)
                total = acc_in[index, which] * jnp.exp2((before - top) * factor)
            for flag, score, value in zip(flags, scores, values):
                shift = top if flag is None else jnp.where(flag, top, ABSENT)
                weights = jnp.exp2((score - shift) * factor).astype(jnp.bfloat16)
                term = jnp.dot(weights, value, preferred_element_type=jnp.float32)
                total = term if total is None else total + term
            if first:
                m_out, acc_out = refs
                m_out[index, which] = jnp.broadcast_to(top, (rows, head_size))
                acc_out[index, which] = total
            else:
                out = refs[2]
                out[:, columns] = (total[:, :head_size] / total[:, head_size:]).astype(jnp.bfloat16)


def attend(times, queries, layers, head_size, carry=None):
    rows, width = queries[0].shape
    heads = width // head_size
    vmem = pl.BlockSpec(memory_space=pltpu.VMEM)
    arguments = [*queries, *layers]
    if carry is None:
        out_shape = [
            jax.ShapeDtypeStruct((heads, 2, rows, head_size), jnp.float32),
            jax.ShapeDtypeStruct((heads, 2, rows, 2 * head_size), jnp.float32),
        ]
        out_specs = [vmem, vmem]
    else:
        arguments += list(carry)
        out_shape = jax.ShapeDtypeStruct((rows, width), jnp.bfloat16)
        out_specs = vmem
    return pl.pallas_call(
        functools.partial(attend_kernel, 1.0 / math.sqrt(head_size), carry is None, head_size, times),
        out_shape=out_shape,
        in_specs=[vmem] * len(arguments),
        out_specs=out_specs,
        compiler_params=pltpu.CompilerParams(vmem_limit_bytes=16 * MIB),
        cost_estimate=pl.CostEstimate(
            flops=heads * len(times) * rows * 3 * rows * head_size * 8,
            bytes_accessed=8 * MIB,
            transcendentals=heads * len(times) * rows * 3 * rows,
        ),
    )(*arguments)


def plane_sum(pieces, weights, spans, write):
    shift = lax.axis_index("row") ^ lax.axis_index("col")
    for case in range(4):

        @pl.when(shift == case)
        def _(case=case):
            for part, (low, high) in enumerate(spans):
                total = None
                for index, piece in enumerate(pieces):
                    term = jnp.dot(piece, weights(index ^ case, part, low, high), preferred_element_type=jnp.float32)
                    total = term if total is None else total + term
                write(part, low, high, total)


def weight_of(kvw, kvw_pair, kvw_mid, inner, forward, outer, which, part):
    if which == 2:
        return inner[part] + forward(part)
    if which == 3:
        return kvw_mid[2 + part] + outer[part][...]
    return (kvw, kvw_pair)[which][2 + part]


def peer_kernel(part, a0, a1, a2, a3, kvw, kvw_pair, kvw_mid, inner, forward, outer, out):
    def write(unused, low, high, total):
        out[...] = total.astype(out.dtype)

    def weights(which, unused, low, high):
        return weight_of(kvw, kvw_pair, kvw_mid, inner, lambda p: forward[...], {part: outer}, which, part)

    plane_sum([a[...] for a in (a0, a1, a2, a3)], weights, [(0, out.shape[1])], write)


def own_kernel(spans, a0, a1, a2, a3, kvw, kvw_pair, kvw_mid, inner, gate, stream_hbm, *rest):
    forward, outer = rest[:2], rest[2 : 4]
    out, stream, sem = rest[4 :]
    copy = pltpu.make_async_copy(stream_hbm, stream, sem)
    copy.start()
    copy.wait()

    def write(part, low, high, total):
        out[:, low:high] = stream[:, low:high].astype(jnp.float32) + gate[:, low:high] * total

    def weights(which, part, low, high):
        return weight_of(kvw, kvw_pair, kvw_mid, inner, lambda p: forward[p][...], outer, which, part)

    plane_sum([a[...] for a in (a0, a1, a2, a3)], weights, spans, write)


def final_kernel(spans, base, gate, *rest):
    received, out_hbm, out, sems = rest[:-3], rest[-3], rest[-2], rest[-1]
    copies = []
    for part, (low, high) in enumerate(spans):
        total = base[:, low:high] + gate[:, low:high] * received[part][...].astype(jnp.float32)
        out[:, low:high] = total.astype(out.dtype)
        copies.append(pltpu.make_async_copy(out.at[:, low:high], out_hbm.at[:, low:high], sems.at[part]))
        copies[-1].start()
    for copy in copies:
        copy.wait()


def pair_body(stream, query_input, key_input, value_input, q_gain, k_gain, out_weight, gate):
    head_size = q_gain.shape[1]
    tokens, width = stream.shape
    rows = lax.axis_size("row")
    spans = [(width * i // CHUNKS, width * (i + 1) // CHUNKS) for i in range(CHUNKS)]

    def swap(x):
        return lax.ppermute(x, "seq", [(0, 1), (1, 0)])

    def pair(x):
        return lax.ppermute(x, "row", [(i, i ^ 1) for i in range(4)])

    def middle(x):
        return lax.ppermute(x, "row", [(1, 2), (2, 1)])

    def along(x, axis, mask):
        return lax.ppermute(x, axis, [(i, i ^ mask) for i in range(4)])

    def call(kernel, arguments, specs, out_shape, out_spec, scratch, flops):
        return pl.pallas_call(
            kernel,
            out_shape=out_shape,
            in_specs=specs,
            out_specs=out_spec,
            scratch_shapes=scratch,
            compiler_params=pltpu.CompilerParams(vmem_limit_bytes=LAST_VMEM),
            cost_estimate=pl.CostEstimate(flops=flops, bytes_accessed=2 * MIB, transcendentals=0),
        )(*arguments)

    def inward(x):
        return lax.ppermute(x, "row", [(1, 0), (2, 3)])

    barrier = lax.optimization_barrier
    kv_send, kvw, q_send, q_keep = prep(query_input, key_input, value_input, q_gain, k_gain, out_weight)
    kv_peer = swap(kv_send)
    kvw_pair, kvw_mid = pair(kvw), middle(kvw)
    q_peer = swap(q_send)
    peer_pair, peer_mid = pair(kv_peer), middle(kv_peer)

    carry = attend((0, 1), [q_keep, q_peer], [kvw, kvw_pair, kvw_mid], head_size)
    first_pair, early_mid, carry = barrier((kvw_pair[2], kvw_mid[2:], carry))
    inner, forwards = inward(early_mid), [middle(first_pair)]
    layers = [kv_peer, peer_pair, peer_mid]
    theirs = attend((1,), [q_peer], layers, head_size, carry)
    across_theirs, beside_theirs = along(theirs, "col", 2), along(theirs, "col", 1)
    next_pair = barrier((kvw_pair[3], theirs))[0]
    forwards.append(middle(next_pair))
    outer = [inward(forwards[part]) for part in range(2)]

    gate = gate.reshape(1, width)
    vmem, hbm = vmem_spec(), hbm_spec()
    groups = [theirs, beside_theirs, across_theirs, along(across_theirs, "col", 1)]
    sents = []
    for part, (low, high) in enumerate(spans):
        sent = call(
            functools.partial(peer_kernel, part),
            [*groups, kvw, kvw_pair, kvw_mid, inner, forwards[part], outer[part]],
            [vmem] * 10,
            jax.ShapeDtypeStruct((tokens, high - low), jnp.bfloat16),
            vmem,
            [],
            tokens * width * (high - low) * 40,
        )
        if part == 0:
            sent, groups[0] = barrier((sent, groups[0]))
        sents.append(sent)
    received = [swap(sent) for sent in sents]
    carry, forwards[1] = barrier((carry, forwards[1]))
    mine = attend((0,), [q_keep], layers, head_size, carry)
    across_mine, beside_mine = along(mine, "col", 2), along(mine, "col", 1)
    groups = [mine, beside_mine, across_mine, along(across_mine, "col", 1)]
    base = call(
        functools.partial(own_kernel, spans),
        [*groups, kvw, kvw_pair, kvw_mid, inner, gate, stream, *forwards, *outer],
        [vmem] * 9 + [hbm] + [vmem] * 4,
        jax.ShapeDtypeStruct((tokens, width), jnp.float32),
        vmem,
        [pltpu.VMEM((tokens, width), stream.dtype), pltpu.SemaphoreType.DMA(())],
        tokens * width * width * 4,
    )
    return call(
        functools.partial(final_kernel, spans),
        [base, gate, *received],
        [vmem] * (2 + CHUNKS),
        jax.ShapeDtypeStruct((tokens, width), jnp.bfloat16),
        hbm,
        [pltpu.VMEM((tokens, width), jnp.bfloat16), pltpu.SemaphoreType.DMA((CHUNKS,))],
        tokens * width * 4,
    )


def solution(mesh):
    placed = (
        P(("seq", "row"), "col"),
        P(("seq", "row"), "col"),
        P(("seq", "row"), "col"),
        P(("seq", "row"), "col"),
        P("col", None),
        P("col", None),
        P("row", "col"),
        P("col"),
    )
    shape = mesh.shape
    paired = shape["seq"] == 2 and shape["row"] == 4 and shape["col"] == 4
    return jax.shard_map(
        pair_body if paired else body, mesh=mesh, in_specs=placed, out_specs=P(("seq", "row"), "col"), check_vma=False
    )
```

```python
import functools
import math

import jax
import jax.numpy as jnp
from jax import lax
from jax.experimental import pallas as pl
from jax.experimental.pallas import tpu as pltpu
from jax.sharding import PartitionSpec as P

EPSILON = 1e-06
NEGATIVE_FLOOR = -1e30


def padded_2(block, sides, width):
    for axis, dim in sides:
        count = lax.axis_size(axis)
        forward = [(i, i + 1) for i in range(count - 1)]
        backward = [(target, source) for source, target in forward]
        low = lax.ppermute(
            lax.slice_in_dim(block, block.shape[dim] - width, None, axis=dim), axis, forward
        )
        high = lax.ppermute(lax.slice_in_dim(block, 0, width, axis=dim), axis, backward)
        block = jnp.concatenate([low, block, high], axis=dim)
    return block


def normalize(values, gain_table):
    token_count = values.shape[0]
    head_count, head_size = gain_table.shape
    split = values.astype(jnp.float32).reshape(token_count, head_count, head_size)
    mean_square = jnp.mean(split * split, axis=-1, keepdims=True)
    return (split * lax.rsqrt(mean_square + EPSILON) * gain_table).astype(jnp.bfloat16)


def layer_terms(queries, key_rows, value_rows, score_scale):
    scores = (
        jnp.einsum("qhd,khd->hqk", queries, key_rows, preferred_element_type=jnp.float32)
        * score_scale
    )
    layer_max = jnp.max(scores, axis=-1)
    unnormed = jnp.exp(scores - layer_max[..., None]).astype(jnp.bfloat16)
    layer_sum = jnp.sum(unnormed.astype(jnp.float32), axis=-1)
    weighted = jnp.einsum("hqk,khd->qhd", unnormed, value_rows, preferred_element_type=jnp.float32)
    return (layer_max, layer_sum, weighted)


def combine(maxima, layer_sums, weighted, presence):
    mask = presence[:, None, None]
    maxima = jnp.where(mask, maxima, NEGATIVE_FLOOR)
    layer_sums = jnp.where(mask, layer_sums, 0.0)
    overall = jnp.max(maxima, axis=0)
    factors = jnp.exp(maxima - overall)
    denominator = jnp.sum(factors * layer_sums, axis=0)
    numerator = jnp.sum(jnp.transpose(factors, (0, 2, 1))[..., None] * weighted, axis=0)
    return numerator / jnp.transpose(denominator)[..., None]


def body(stream, query_input, key_input, value_input, q_gain, k_gain, out_weight, gate):
    token_count, feature_count = query_input.shape
    head_count, head_size = q_gain.shape
    score_scale = 1.0 / math.sqrt(head_size)
    queries = normalize(query_input, q_gain)
    normed_keys = normalize(key_input, k_gain).reshape(token_count, feature_count)
    layered = jnp.stack([normed_keys, value_input], axis=0)[None, None]
    padded = padded_2(layered, (("seq", 0), ("row", 1)), 1)
    padded = padded.reshape(9, 2, token_count, feature_count)
    key_stack = padded[:, 0].reshape(9, token_count, head_count, head_size)
    value_stack = padded[:, 1].reshape(9, token_count, head_count, head_size)
    time_index = lax.axis_index("seq")
    time_count = lax.axis_size("seq")
    height_index = lax.axis_index("row")
    height_count = lax.axis_size("row")
    time_present = [time_index > 0, time_index >= 0, time_index < time_count - 1]
    height_present = [height_index > 0, height_index >= 0, height_index < height_count - 1]
    presence = jnp.stack(
        [time_flag & height_flag for time_flag in time_present for height_flag in height_present]
    )
    result_set = [
        layer_terms(queries, key_stack[layer_index], value_stack[layer_index], score_scale)
        for layer_index in range(9)
    ]
    maxima = jnp.stack([entry[0] for entry in result_set])
    layer_sums = jnp.stack([entry[1] for entry in result_set])
    weighted = jnp.stack([entry[2] for entry in result_set])
    attention = (
        combine(maxima, layer_sums, weighted, presence)
        .reshape(token_count, feature_count)
        .astype(jnp.bfloat16)
    )
    all_heads = lax.all_gather(attention, "col", axis=1, tiled=True)
    projected = jnp.dot(
        all_heads,
        lax.all_gather(out_weight, "row", axis=0, tiled=True),
        preferred_element_type=jnp.float32,
    )
    return (stream.astype(jnp.float32) + gate * projected).astype(jnp.bfloat16)


ABSENT = 1e30
LOG2_E = 1.4426950408889634
MIB = 1 << 20
CUT = 3
FIRST_VMEM = 60 * MIB
LAST_VMEM = 16 * MIB


def vmem_spec():
    return pl.BlockSpec(memory_space=pltpu.VMEM)


def hbm_spec():
    return pl.BlockSpec(memory_space=pltpu.HBM)


def normed(ref, gain_ref, part, out):
    head_size = gain_ref.shape[1]
    half = out.shape[1]
    count = half // head_size
    for index in range(count):
        start = pl.multiple_of(part * half + index * head_size, head_size)
        x = ref[:, pl.ds(start, head_size)].astype(jnp.float32)
        mean_square = jnp.mean(x * x, axis=-1, keepdims=True)
        gain = gain_ref[pl.ds(part * count + index, 1), :]
        scaled = x * lax.rsqrt(mean_square + EPSILON) * gain
        out[:, index * head_size : (index + 1) * head_size] = scaled.astype(jnp.bfloat16)


def prep_kernel(
    k_hbm, v_hbm, kg_hbm, w_hbm, kv_send, kvw_keep, k_ref, kg_ref, sems
):
    mine = lax.axis_index("seq")
    half = kv_send.shape[1] // 2
    rows = pl.ds(pl.multiple_of(mine * half, half), half)
    moved = [(kg_hbm, kg_ref), (k_hbm, k_ref)]
    for part, out in ((1 - mine, kv_send), (mine, kvw_keep)):
        moved.append((v_hbm.at[:, pl.ds(pl.multiple_of(part * half, half), half)], out.at[:, half : 2 * half]))
    moved.append((w_hbm.at[rows, :], kvw_keep.at[:, 2 * half :]))
    copies = [
        pltpu.make_async_copy(source, target, sems.at[index]) for index, (source, target) in enumerate(moved)
    ]
    for copy in copies:
        copy.start()

    copies[0].wait()
    copies[1].wait()
    for part, kv_out in ((1 - mine, kv_send), (mine, kvw_keep)):
        normed(k_ref, kg_ref, part, kv_out.at[:, :half])
    for copy in copies[2:]:
        copy.wait()


def query_kernel(q_hbm, qg_hbm, q_send, q_keep, q_ref, qg_ref, sems):
    mine = lax.axis_index("seq")
    copies = [
        pltpu.make_async_copy(qg_hbm, qg_ref, sems.at[0]),
        pltpu.make_async_copy(q_hbm, q_ref, sems.at[1]),
    ]
    for copy in copies:
        copy.start()
    for copy in copies:
        copy.wait()
    for part, q_out in ((1 - mine, q_send), (mine, q_keep)):
        normed(q_ref, qg_ref, part, q_out)


def prep(q, k, v, q_gain, k_gain, out_weight):
    rows, width = q.shape
    half = width // 2
    one = jax.ShapeDtypeStruct((rows, half), jnp.bfloat16)
    two = jax.ShapeDtypeStruct((rows, width), jnp.bfloat16)
    four = jax.ShapeDtypeStruct((rows, width + out_weight.shape[1]), jnp.bfloat16)
    block = pltpu.VMEM((rows, width), jnp.bfloat16)
    gain = pltpu.VMEM(q_gain.shape, jnp.float32)
    params = pltpu.CompilerParams(vmem_limit_bytes=FIRST_VMEM)
    cost = pl.CostEstimate(flops=rows * width * 8, bytes_accessed=rows * width * 6, transcendentals=0)
    kv_send, kvw = pl.pallas_call(
        prep_kernel,
        out_shape=[two, four],
        in_specs=[hbm_spec()] * 4,
        out_specs=[vmem_spec()] * 2,
        scratch_shapes=[block, gain, pltpu.SemaphoreType.DMA((5,))],
        compiler_params=params,
        cost_estimate=cost,
    )(k, v, k_gain, out_weight)
    kvw, q = lax.optimization_barrier((kvw, q))
    q_send, q_keep = pl.pallas_call(
        query_kernel,
        out_shape=[one, one],
        in_specs=[hbm_spec()] * 2,
        out_specs=[vmem_spec()] * 2,
        scratch_shapes=[block, gain, pltpu.SemaphoreType.DMA((2,))],
        compiler_params=pltpu.CompilerParams(vmem_limit_bytes=LAST_VMEM),
        cost_estimate=cost,
    )(q, q_gain)
    return kv_send, kvw, q_send, q_keep


def attend_kernel(scale, first, head_size, times, *refs):
    queries, refs = refs[: len(times)], refs[len(times) :]
    kv0, kv1, kv2 = refs[:3]
    refs = refs[3:]
    height = lax.axis_index("row")
    flags = [None, None, (height > 0) & (height < lax.axis_size("row") - 1)]
    rows, half = queries[0].shape
    factor = scale * LOG2_E
    ones = jnp.ones((rows, head_size), jnp.bfloat16)

    for index in range(queries[0].shape[1] // head_size):
        columns = slice(index * head_size, (index + 1) * head_size)
        beside = slice(half + index * head_size, half + (index + 1) * head_size)
        keys = [kv[:, columns] for kv in (kv0, kv1, kv2)]
        values = [jnp.concatenate([kv[:, beside], ones], axis=1) for kv in (kv0, kv1, kv2)]
        for which, q_ref in zip(times, queries):
            q = q_ref[:, columns]
            scores = [
                lax.dot_general(q, key, (((1,), (1,)), ((), ())), preferred_element_type=jnp.float32)
                for key in keys
            ]
            top = None
            for flag, score in zip(flags, scores):
                part = score[:, :head_size]
                for start in range(head_size, rows, head_size):
                    part = jnp.maximum(part, score[:, start : start + head_size])
                if flag is not None:
                    part = jnp.where(flag, part, NEGATIVE_FLOOR)
                top = part if top is None else jnp.maximum(top, part)
            top = jnp.max(top, axis=1, keepdims=True)
            total = None
            if not first:
                m_in, acc_in = refs[:2]
                before = m_in[index, which][:, :1]
                top = jnp.maximum(before, top)
                total = acc_in[index, which] * jnp.exp2((before - top) * factor)
            for flag, score, value in zip(flags, scores, values):
                shift = top if flag is None else jnp.where(flag, top, ABSENT)
                weights = jnp.exp2((score - shift) * factor).astype(jnp.bfloat16)
                term = jnp.dot(weights, value, preferred_element_type=jnp.float32)
                total = term if total is None else total + term
            if first:
                m_out, acc_out = refs
                m_out[index, which] = jnp.broadcast_to(top, (rows, head_size))
                acc_out[index, which] = total
            else:
                out = refs[2]
                out[:, columns] = (total[:, :head_size] / total[:, head_size:]).astype(jnp.bfloat16)


def attend(times, queries, layers, head_size, carry=None):
    rows, width = queries[0].shape
    heads = width // head_size
    vmem = pl.BlockSpec(memory_space=pltpu.VMEM)
    arguments = [*queries, *layers]
    if carry is None:
        out_shape = [
            jax.ShapeDtypeStruct((heads, 2, rows, head_size), jnp.float32),
            jax.ShapeDtypeStruct((heads, 2, rows, 2 * head_size), jnp.float32),
        ]
        out_specs = [vmem, vmem]
    else:
        arguments += list(carry)
        out_shape = jax.ShapeDtypeStruct((rows, width), jnp.bfloat16)
        out_specs = vmem
    return pl.pallas_call(
        functools.partial(attend_kernel, 1.0 / math.sqrt(head_size), carry is None, head_size, times),
        out_shape=out_shape,
        in_specs=[vmem] * len(arguments),
        out_specs=out_specs,
        compiler_params=pltpu.CompilerParams(vmem_limit_bytes=16 * MIB),
        cost_estimate=pl.CostEstimate(
            flops=heads * len(times) * rows * 3 * rows * head_size * 8,
            bytes_accessed=8 * MIB,
            transcendentals=heads * len(times) * rows * 3 * rows,
        ),
    )(*arguments)


def plane_sum(pieces, weights, spans, write):
    shift = lax.axis_index("row") ^ lax.axis_index("col")
    for case in range(4):

        @pl.when(shift == case)
        def _(case=case):
            for part, (low, high) in enumerate(spans):
                total = None
                for index, piece in enumerate(pieces):
                    term = jnp.dot(piece, weights(index ^ case, part, low, high), preferred_element_type=jnp.float32)
                    total = term if total is None else total + term
                write(part, low, high, total)


def weight_of(kvw, kvw_pair, kvw_mid, inner, forward, outer, which, low, high):
    start = kvw.shape[1] - kvw.shape[0] * 2
    columns = slice(start + low, start + high)
    if which == 2:
        return inner + forward
    if which == 3:
        return kvw_mid[:, columns] + outer
    return (kvw, kvw_pair)[which][:, columns]


def peer_kernel(span, a0, a1, a2, a3, kvw, kvw_pair, kvw_mid, inner, forward, outer, out):
    def write(part, low, high, total):
        out[...] = total.astype(out.dtype)

    def weights(which, part, low, high):
        held = inner[:, slice(*span)], forward[...], outer[...]
        return weight_of(kvw, kvw_pair, kvw_mid, *held, which, low, high)

    plane_sum([a[...] for a in (a0, a1, a2, a3)], weights, [span], write)


def own_kernel(spans, a0, a1, a2, a3, kvw, kvw_pair, kvw_mid, gate, stream_hbm, *rest):
    forward, outer, inner = rest[:2], rest[2:4], rest[4:-3]
    out, stream, sem = rest[-3:]
    copy = pltpu.make_async_copy(stream_hbm, stream, sem)
    copy.start()
    copy.wait()

    def write(part, low, high, total):
        out[:, low:high] = stream[:, low:high].astype(jnp.float32) + gate[:, low:high] * total

    def weights(which, part, low, high):
        held = inner[0][:, low:high], forward[part][...], outer[part][...]
        return weight_of(kvw, kvw_pair, kvw_mid, *held, which, low, high)

    plane_sum([a[...] for a in (a0, a1, a2, a3)], weights, spans, write)


def final_kernel(spans, base, gate, *rest):
    received, out_hbm, out, sems = rest[:-3], rest[-3], rest[-2], rest[-1]
    copies = []
    for part, (low, high) in enumerate(spans):
        total = base[:, low:high] + gate[:, low:high] * received[part][...].astype(jnp.float32)
        out[:, low:high] = total.astype(out.dtype)
        copies.append(pltpu.make_async_copy(out.at[:, low:high], out_hbm.at[:, low:high], sems.at[part]))
        copies[-1].start()
    for copy in copies:
        copy.wait()


def pair_body(stream, query_input, key_input, value_input, q_gain, k_gain, out_weight, gate):
    head_size = q_gain.shape[1]
    tokens, width = stream.shape
    rows = lax.axis_size("row")
    cut = width // 6 * CUT
    spans = [(0, cut), (cut, width)]

    def swap(x):
        return lax.ppermute(x, "seq", [(0, 1), (1, 0)])

    def pair(x):
        return lax.ppermute(x, "row", [(i, i ^ 1) for i in range(4)])

    def middle(x):
        return lax.ppermute(x, "row", [(1, 2), (2, 1)])

    def along(x, axis, mask):
        return lax.ppermute(x, axis, [(i, i ^ mask) for i in range(4)])

    def call(kernel, arguments, specs, out_shape, out_spec, scratch, flops):
        return pl.pallas_call(
            kernel,
            out_shape=out_shape,
            in_specs=specs,
            out_specs=out_spec,
            scratch_shapes=scratch,
            compiler_params=pltpu.CompilerParams(vmem_limit_bytes=LAST_VMEM),
            cost_estimate=pl.CostEstimate(flops=flops, bytes_accessed=2 * MIB, transcendentals=0),
        )(*arguments)

    def inward(x):
        return lax.ppermute(x, "row", [(1, 0), (2, 3)])

    barrier = lax.optimization_barrier
    kv_send, kvw, q_send, q_keep = prep(query_input, key_input, value_input, q_gain, k_gain, out_weight)
    kv_peer = swap(kv_send)
    kvw_pair, kvw_mid = pair(kvw), middle(kvw)
    q_peer = swap(q_send)
    peer_pair, peer_mid = pair(kv_peer), middle(kv_peer)

    carry = attend((0, 1), [q_keep, q_peer], [kvw, kvw_pair, kvw_mid], head_size)
    starts = [width + low for low, high in spans] + [2 * width]
    halves = [slice(starts[part], starts[part + 1]) for part in range(2)]
    first_pair, early_mid, carry = barrier((kvw_pair[:, halves[0]], kvw_mid[:, width:], carry))
    inner, forwards = [inward(early_mid)], [middle(first_pair)]
    layers = [kv_peer, peer_pair, peer_mid]
    theirs = attend((1,), [q_peer], layers, head_size, carry)
    across_theirs, beside_theirs = along(theirs, "col", 2), along(theirs, "col", 1)
    next_pair, _ = barrier((kvw_pair[:, halves[1]], theirs))
    forwards.append(middle(next_pair))
    outer = [inward(forwards[part]) for part in range(2)]

    gate = gate.reshape(1, width)
    vmem, hbm = vmem_spec(), hbm_spec()
    groups = [theirs, beside_theirs, across_theirs, along(across_theirs, "col", 1)]
    sents = []
    for part, (low, high) in enumerate(spans):
        sent = call(
            functools.partial(peer_kernel, (low, high)),
            [*groups, kvw, kvw_pair, kvw_mid, inner[0], forwards[part], outer[part]],
            [vmem] * 10,
            jax.ShapeDtypeStruct((tokens, high - low), jnp.bfloat16),
            vmem,
            [],
            tokens * width * (high - low) * 40,
        )
        if part == 0:
            sent, groups[0] = barrier((sent, groups[0]))
        sents.append(sent)
    received = [swap(sent) for sent in sents]
    carry, forwards[1], inner[0] = barrier((carry, forwards[1], inner[0]))
    mine = attend((0,), [q_keep], layers, head_size, carry)
    across_mine, beside_mine = along(mine, "col", 2), along(mine, "col", 1)
    groups = [mine, beside_mine, across_mine, along(across_mine, "col", 1)]
    base = call(
        functools.partial(own_kernel, spans),
        [*groups, kvw, kvw_pair, kvw_mid, gate, stream, *forwards, *outer, *inner],
        [vmem] * 8 + [hbm] + [vmem] * (4 + len(inner)),
        jax.ShapeDtypeStruct((tokens, width), jnp.float32),
        vmem,
        [pltpu.VMEM((tokens, width), stream.dtype), pltpu.SemaphoreType.DMA(())],
        tokens * width * width * 4,
    )
    return call(
        functools.partial(final_kernel, spans),
        [base, gate, *received],
        [vmem] * (2 + len(received)),
        jax.ShapeDtypeStruct((tokens, width), jnp.bfloat16),
        hbm,
        [pltpu.VMEM((tokens, width), jnp.bfloat16), pltpu.SemaphoreType.DMA((len(spans),))],
        tokens * width * 4,
    )


def solution(mesh):
    placed = (
        P(("seq", "row"), "col"),
        P(("seq", "row"), "col"),
        P(("seq", "row"), "col"),
        P(("seq", "row"), "col"),
        P("col", None),
        P("col", None),
        P("row", "col"),
        P("col"),
    )
    shape = mesh.shape
    paired = shape["seq"] == 2 and shape["row"] == 4 and shape["col"] == 4
    return jax.shard_map(
        pair_body if paired else body, mesh=mesh, in_specs=placed, out_specs=P(("seq", "row"), "col"), check_vma=False
    )
```

```python
import functools
import math

import jax
import jax.numpy as jnp
from jax import lax
from jax.experimental import pallas as pl
from jax.experimental.pallas import tpu as pltpu
from jax.sharding import PartitionSpec as P

EPSILON = 1e-06
NEGATIVE_FLOOR = -1e30


def padded_2(block, sides, width):
    for axis, dim in sides:
        count = lax.axis_size(axis)
        forward = [(i, i + 1) for i in range(count - 1)]
        backward = [(target, source) for source, target in forward]
        low = lax.ppermute(
            lax.slice_in_dim(block, block.shape[dim] - width, None, axis=dim), axis, forward
        )
        high = lax.ppermute(lax.slice_in_dim(block, 0, width, axis=dim), axis, backward)
        block = jnp.concatenate([low, block, high], axis=dim)
    return block


def normalize(values, gain_table):
    token_count = values.shape[0]
    head_count, head_size = gain_table.shape
    split = values.astype(jnp.float32).reshape(token_count, head_count, head_size)
    mean_square = jnp.mean(split * split, axis=-1, keepdims=True)
    return (split * lax.rsqrt(mean_square + EPSILON) * gain_table).astype(jnp.bfloat16)


def layer_terms(queries, key_rows, value_rows, score_scale):
    scores = (
        jnp.einsum("qhd,khd->hqk", queries, key_rows, preferred_element_type=jnp.float32)
        * score_scale
    )
    layer_max = jnp.max(scores, axis=-1)
    unnormed = jnp.exp(scores - layer_max[..., None]).astype(jnp.bfloat16)
    layer_sum = jnp.sum(unnormed.astype(jnp.float32), axis=-1)
    weighted = jnp.einsum("hqk,khd->qhd", unnormed, value_rows, preferred_element_type=jnp.float32)
    return (layer_max, layer_sum, weighted)


def combine(maxima, layer_sums, weighted, presence):
    mask = presence[:, None, None]
    maxima = jnp.where(mask, maxima, NEGATIVE_FLOOR)
    layer_sums = jnp.where(mask, layer_sums, 0.0)
    overall = jnp.max(maxima, axis=0)
    factors = jnp.exp(maxima - overall)
    denominator = jnp.sum(factors * layer_sums, axis=0)
    numerator = jnp.sum(jnp.transpose(factors, (0, 2, 1))[..., None] * weighted, axis=0)
    return numerator / jnp.transpose(denominator)[..., None]


def body(stream, query_input, key_input, value_input, q_gain, k_gain, out_weight, gate):
    token_count, feature_count = query_input.shape
    head_count, head_size = q_gain.shape
    score_scale = 1.0 / math.sqrt(head_size)
    queries = normalize(query_input, q_gain)
    normed_keys = normalize(key_input, k_gain).reshape(token_count, feature_count)
    layered = jnp.stack([normed_keys, value_input], axis=0)[None, None]
    padded = padded_2(layered, (("seq", 0), ("row", 1)), 1)
    padded = padded.reshape(9, 2, token_count, feature_count)
    key_stack = padded[:, 0].reshape(9, token_count, head_count, head_size)
    value_stack = padded[:, 1].reshape(9, token_count, head_count, head_size)
    time_index = lax.axis_index("seq")
    time_count = lax.axis_size("seq")
    height_index = lax.axis_index("row")
    height_count = lax.axis_size("row")
    time_present = [time_index > 0, time_index >= 0, time_index < time_count - 1]
    height_present = [height_index > 0, height_index >= 0, height_index < height_count - 1]
    presence = jnp.stack(
        [time_flag & height_flag for time_flag in time_present for height_flag in height_present]
    )
    result_set = [
        layer_terms(queries, key_stack[layer_index], value_stack[layer_index], score_scale)
        for layer_index in range(9)
    ]
    maxima = jnp.stack([entry[0] for entry in result_set])
    layer_sums = jnp.stack([entry[1] for entry in result_set])
    weighted = jnp.stack([entry[2] for entry in result_set])
    attention = (
        combine(maxima, layer_sums, weighted, presence)
        .reshape(token_count, feature_count)
        .astype(jnp.bfloat16)
    )
    all_heads = lax.all_gather(attention, "col", axis=1, tiled=True)
    projected = jnp.dot(
        all_heads,
        lax.all_gather(out_weight, "row", axis=0, tiled=True),
        preferred_element_type=jnp.float32,
    )
    return (stream.astype(jnp.float32) + gate * projected).astype(jnp.bfloat16)


ABSENT = 1e30
LOG2_E = 1.4426950408889634
MIB = 1 << 20
CUT = 3
FIRST_VMEM = 60 * MIB
LAST_VMEM = 16 * MIB


def vmem_spec():
    return pl.BlockSpec(memory_space=pltpu.VMEM)


def hbm_spec():
    return pl.BlockSpec(memory_space=pltpu.HBM)


def normed(ref, gain_ref, part, out):
    head_size = gain_ref.shape[1]
    half = out.shape[1]
    count = half // head_size
    for index in range(count):
        start = pl.multiple_of(part * half + index * head_size, head_size)
        x = ref[:, pl.ds(start, head_size)].astype(jnp.float32)
        mean_square = jnp.mean(x * x, axis=-1, keepdims=True)
        gain = gain_ref[pl.ds(part * count + index, 1), :]
        scaled = x * lax.rsqrt(mean_square + EPSILON) * gain
        out[:, index * head_size : (index + 1) * head_size] = scaled.astype(jnp.bfloat16)


def prep_kernel(
    k_hbm, v_hbm, kg_hbm, w_hbm, kv_send, kvw_keep, k_ref, kg_ref, sems
):
    mine = lax.axis_index("seq")
    half = kv_send.shape[1] // 2
    rows = pl.ds(pl.multiple_of(mine * half, half), half)
    moved = [(kg_hbm, kg_ref), (k_hbm, k_ref)]
    for part, out in ((1 - mine, kv_send), (mine, kvw_keep)):
        moved.append((v_hbm.at[:, pl.ds(pl.multiple_of(part * half, half), half)], out.at[:, half : 2 * half]))
    moved.append((w_hbm.at[rows, :], kvw_keep.at[:, 2 * half :]))
    copies = [
        pltpu.make_async_copy(source, target, sems.at[index]) for index, (source, target) in enumerate(moved)
    ]
    for copy in copies:
        copy.start()

    copies[0].wait()
    copies[1].wait()
    for part, kv_out in ((1 - mine, kv_send), (mine, kvw_keep)):
        normed(k_ref, kg_ref, part, kv_out.at[:, :half])
    for copy in copies[2:]:
        copy.wait()


def query_kernel(q_hbm, qg_hbm, q_send, q_keep, q_ref, qg_ref, sems):
    mine = lax.axis_index("seq")
    copies = [
        pltpu.make_async_copy(qg_hbm, qg_ref, sems.at[0]),
        pltpu.make_async_copy(q_hbm, q_ref, sems.at[1]),
    ]
    for copy in copies:
        copy.start()
    for copy in copies:
        copy.wait()
    for part, q_out in ((1 - mine, q_send), (mine, q_keep)):
        normed(q_ref, qg_ref, part, q_out)


def prep(q, k, v, q_gain, k_gain, out_weight):
    rows, width = q.shape
    half = width // 2
    one = jax.ShapeDtypeStruct((rows, half), jnp.bfloat16)
    two = jax.ShapeDtypeStruct((rows, width), jnp.bfloat16)
    four = jax.ShapeDtypeStruct((rows, width + out_weight.shape[1]), jnp.bfloat16)
    block = pltpu.VMEM((rows, width), jnp.bfloat16)
    gain = pltpu.VMEM(q_gain.shape, jnp.float32)
    params = pltpu.CompilerParams(vmem_limit_bytes=FIRST_VMEM)
    cost = pl.CostEstimate(flops=rows * width * 8, bytes_accessed=rows * width * 6, transcendentals=0)
    kv_send, kvw = pl.pallas_call(
        prep_kernel,
        out_shape=[two, four],
        in_specs=[hbm_spec()] * 4,
        out_specs=[vmem_spec()] * 2,
        scratch_shapes=[block, gain, pltpu.SemaphoreType.DMA((5,))],
        compiler_params=params,
        cost_estimate=cost,
    )(k, v, k_gain, out_weight)
    kvw, q = lax.optimization_barrier((kvw, q))
    q_send, q_keep = pl.pallas_call(
        query_kernel,
        out_shape=[one, one],
        in_specs=[hbm_spec()] * 2,
        out_specs=[vmem_spec()] * 2,
        scratch_shapes=[block, gain, pltpu.SemaphoreType.DMA((2,))],
        compiler_params=pltpu.CompilerParams(vmem_limit_bytes=LAST_VMEM),
        cost_estimate=cost,
    )(q, q_gain)
    return kv_send, kvw, q_send, q_keep


def attend_kernel(scale, first, head_size, times, *refs):
    queries, refs = refs[: len(times)], refs[len(times) :]
    kv0, kv1, kv2 = refs[:3]
    refs = refs[3:]
    height = lax.axis_index("row")
    flags = [None, None, (height > 0) & (height < lax.axis_size("row") - 1)]
    rows, half = queries[0].shape
    factor = scale * LOG2_E
    ones = jnp.ones((rows, head_size), jnp.bfloat16)

    for index in range(queries[0].shape[1] // head_size):
        columns = slice(index * head_size, (index + 1) * head_size)
        beside = slice(half + index * head_size, half + (index + 1) * head_size)
        keys = [kv[:, columns] for kv in (kv0, kv1, kv2)]
        values = [jnp.concatenate([kv[:, beside], ones], axis=1) for kv in (kv0, kv1, kv2)]
        for which, q_ref in zip(times, queries):
            q = q_ref[:, columns]
            scores = [
                lax.dot_general(q, key, (((1,), (1,)), ((), ())), preferred_element_type=jnp.float32)
                for key in keys
            ]
            top = None
            for flag, score in zip(flags, scores):
                part = score[:, :head_size]
                for start in range(head_size, rows, head_size):
                    part = jnp.maximum(part, score[:, start : start + head_size])
                if flag is not None:
                    part = jnp.where(flag, part, NEGATIVE_FLOOR)
                top = part if top is None else jnp.maximum(top, part)
            top = jnp.max(top, axis=1, keepdims=True)
            total = None
            if not first:
                m_in, acc_in = refs[:2]
                before = m_in[index, which][:, :1]
                top = jnp.maximum(before, top)
                total = acc_in[index, which] * jnp.exp2((before - top) * factor)
            for flag, score, value in zip(flags, scores, values):
                shift = top if flag is None else jnp.where(flag, top, ABSENT)
                weights = jnp.exp2((score - shift) * factor).astype(jnp.bfloat16)
                term = jnp.dot(weights, value, preferred_element_type=jnp.float32)
                total = term if total is None else total + term
            if first:
                m_out, acc_out = refs
                m_out[index, which] = jnp.broadcast_to(top, (rows, head_size))
                acc_out[index, which] = total
            else:
                out = refs[2]
                out[:, columns] = (total[:, :head_size] / total[:, head_size:]).astype(jnp.bfloat16)


def attend(times, queries, layers, head_size, carry=None):
    rows, width = queries[0].shape
    heads = width // head_size
    vmem = pl.BlockSpec(memory_space=pltpu.VMEM)
    arguments = [*queries, *layers]
    if carry is None:
        out_shape = [
            jax.ShapeDtypeStruct((heads, 2, rows, head_size), jnp.float32),
            jax.ShapeDtypeStruct((heads, 2, rows, 2 * head_size), jnp.float32),
        ]
        out_specs = [vmem, vmem]
    else:
        arguments += list(carry)
        out_shape = jax.ShapeDtypeStruct((rows, width), jnp.bfloat16)
        out_specs = vmem
    return pl.pallas_call(
        functools.partial(attend_kernel, 1.0 / math.sqrt(head_size), carry is None, head_size, times),
        out_shape=out_shape,
        in_specs=[vmem] * len(arguments),
        out_specs=out_specs,
        compiler_params=pltpu.CompilerParams(vmem_limit_bytes=16 * MIB),
        cost_estimate=pl.CostEstimate(
            flops=heads * len(times) * rows * 3 * rows * head_size * 8,
            bytes_accessed=8 * MIB,
            transcendentals=heads * len(times) * rows * 3 * rows,
        ),
    )(*arguments)


def plane_sum(pieces, weights, spans, write):
    shift = lax.axis_index("row") ^ lax.axis_index("col")
    for case in range(4):

        @pl.when(shift == case)
        def _(case=case):
            for part, (low, high) in enumerate(spans):
                total = None
                for index, piece in enumerate(pieces):
                    term = jnp.dot(piece, weights(index ^ case, part, low, high), preferred_element_type=jnp.float32)
                    total = term if total is None else total + term
                write(part, low, high, total)


def weight_of(kvw, kvw_pair, kvw_mid, inner, forward, outer, which, low, high):
    start = kvw.shape[1] - kvw.shape[0] * 2
    columns = slice(start + low, start + high)
    if which == 2:
        return inner + forward
    if which == 3:
        return kvw_mid[:, columns] + outer
    return (kvw, kvw_pair)[which][:, columns]


def peer_kernel(span, a0, a1, a2, a3, kvw, kvw_pair, kvw_mid, inner, forward, outer, out):
    def write(part, low, high, total):
        out[...] = total.astype(out.dtype)

    def weights(which, part, low, high):
        held = inner[:, slice(*span)], forward[...], outer[...]
        return weight_of(kvw, kvw_pair, kvw_mid, *held, which, low, high)

    plane_sum([a[...] for a in (a0, a1, a2, a3)], weights, [span], write)


def own_kernel(spans, a0, a1, a2, a3, kvw, kvw_pair, kvw_mid, gate, stream_hbm, *rest):
    forward, outer, inner = rest[:2], rest[2:4], rest[4:-3]
    out, stream, sem = rest[-3:]
    copy = pltpu.make_async_copy(stream_hbm, stream, sem)
    copy.start()
    copy.wait()

    def write(part, low, high, total):
        out[:, low:high] = stream[:, low:high].astype(jnp.float32) + gate[:, low:high] * total

    def weights(which, part, low, high):
        held = inner[0][:, low:high], forward[part][...], outer[part][...]
        return weight_of(kvw, kvw_pair, kvw_mid, *held, which, low, high)

    plane_sum([a[...] for a in (a0, a1, a2, a3)], weights, spans, write)


def final_kernel(spans, base, gate, *rest):
    received, out_hbm, out, sems = rest[:-3], rest[-3], rest[-2], rest[-1]
    copies = []
    for part, (low, high) in enumerate(spans):
        total = base[:, low:high] + gate[:, low:high] * received[part][...].astype(jnp.float32)
        out[:, low:high] = total.astype(out.dtype)
        copies.append(pltpu.make_async_copy(out.at[:, low:high], out_hbm.at[:, low:high], sems.at[part]))
        copies[-1].start()
    for copy in copies:
        copy.wait()


def pair_body(stream, query_input, key_input, value_input, q_gain, k_gain, out_weight, gate):
    head_size = q_gain.shape[1]
    tokens, width = stream.shape
    rows = lax.axis_size("row")
    cut = width // 6 * CUT
    spans = [(0, cut), (cut, width)]

    def swap(x):
        return lax.ppermute(x, "seq", [(0, 1), (1, 0)])

    def pair(x):
        return lax.ppermute(x, "row", [(i, i ^ 1) for i in range(4)])

    def middle(x):
        return lax.ppermute(x, "row", [(1, 2), (2, 1)])

    def along(x, axis, mask):
        return lax.ppermute(x, axis, [(i, i ^ mask) for i in range(4)])

    def call(kernel, arguments, specs, out_shape, out_spec, scratch, flops):
        return pl.pallas_call(
            kernel,
            out_shape=out_shape,
            in_specs=specs,
            out_specs=out_spec,
            scratch_shapes=scratch,
            compiler_params=pltpu.CompilerParams(vmem_limit_bytes=LAST_VMEM),
            cost_estimate=pl.CostEstimate(flops=flops, bytes_accessed=2 * MIB, transcendentals=0),
        )(*arguments)

    def inward(x):
        return lax.ppermute(x, "row", [(1, 0), (2, 3)])

    barrier = lax.optimization_barrier
    kv_send, kvw, q_send, q_keep = prep(query_input, key_input, value_input, q_gain, k_gain, out_weight)
    kv_peer = swap(kv_send)
    kvw_pair, kvw_mid = pair(kvw), middle(kvw)
    q_peer = swap(q_send)
    peer_pair, peer_mid = pair(kv_peer), middle(kv_peer)

    carry = attend((0, 1), [q_keep, q_peer], [kvw, kvw_pair, kvw_mid], head_size)
    starts = [width + low for low, high in spans] + [2 * width]
    halves = [slice(starts[part], starts[part + 1]) for part in range(2)]
    first_pair, early_mid, carry = barrier((kvw_pair[:, halves[0]], kvw_mid[:, width:], carry))
    inner, forwards = [inward(early_mid)], [middle(first_pair)]
    layers = [kv_peer, peer_pair, peer_mid]
    theirs = attend((1,), [q_peer], layers, head_size, carry)
    across_theirs, beside_theirs = along(theirs, "col", 2), along(theirs, "col", 1)
    next_pair, _ = barrier((kvw_pair[:, halves[1]], theirs))
    forwards.append(middle(next_pair))
    outer = [inward(forwards[part]) for part in range(2)]

    gate = gate.reshape(1, width)
    vmem, hbm = vmem_spec(), hbm_spec()
    groups = [theirs, beside_theirs, across_theirs, along(across_theirs, "col", 1)]
    sents = []
    for part, (low, high) in enumerate(spans):
        sent = call(
            functools.partial(peer_kernel, (low, high)),
            [*groups, kvw, kvw_pair, kvw_mid, inner[0], forwards[part], outer[part]],
            [vmem] * 10,
            jax.ShapeDtypeStruct((tokens, high - low), jnp.bfloat16),
            vmem,
            [],
            tokens * width * (high - low) * 40,
        )
        if part == 0:
            sent, groups[0] = barrier((sent, groups[0]))
        sents.append(sent)
    received = [swap(sent) for sent in sents]
    carry, forwards[1], inner[0] = barrier((carry, forwards[1], inner[0]))
    mine = attend((0,), [q_keep], layers, head_size, carry)
    beside_mine = along(mine, "col", 1)
    across_mine = along(mine, "col", 2)
    groups = [mine, beside_mine, across_mine, along(beside_mine, "col", 2)]
    base = call(
        functools.partial(own_kernel, spans),
        [*groups, kvw, kvw_pair, kvw_mid, gate, stream, *forwards, *outer, *inner],
        [vmem] * 8 + [hbm] + [vmem] * (4 + len(inner)),
        jax.ShapeDtypeStruct((tokens, width), jnp.float32),
        vmem,
        [pltpu.VMEM((tokens, width), stream.dtype), pltpu.SemaphoreType.DMA(())],
        tokens * width * width * 4,
    )
    return call(
        functools.partial(final_kernel, spans),
        [base, gate, *received],
        [vmem] * (2 + len(received)),
        jax.ShapeDtypeStruct((tokens, width), jnp.bfloat16),
        hbm,
        [pltpu.VMEM((tokens, width), jnp.bfloat16), pltpu.SemaphoreType.DMA((len(spans),))],
        tokens * width * 4,
    )


def solution(mesh):
    placed = (
        P(("seq", "row"), "col"),
        P(("seq", "row"), "col"),
        P(("seq", "row"), "col"),
        P(("seq", "row"), "col"),
        P("col", None),
        P("col", None),
        P("row", "col"),
        P("col"),
    )
    shape = mesh.shape
    paired = shape["seq"] == 2 and shape["row"] == 4 and shape["col"] == 4
    return jax.shard_map(
        pair_body if paired else body, mesh=mesh, in_specs=placed, out_specs=P(("seq", "row"), "col"), check_vma=False
    )
```

```python
import functools
import math

import jax
import jax.numpy as jnp
from jax import lax
from jax.experimental import pallas as pl
from jax.experimental.pallas import tpu as pltpu
from jax.sharding import PartitionSpec as P

EPSILON = 1e-06
NEGATIVE_FLOOR = -1e30


def padded_2(block, sides, width):
    for axis, dim in sides:
        count = lax.axis_size(axis)
        forward = [(i, i + 1) for i in range(count - 1)]
        backward = [(target, source) for source, target in forward]
        low = lax.ppermute(
            lax.slice_in_dim(block, block.shape[dim] - width, None, axis=dim), axis, forward
        )
        high = lax.ppermute(lax.slice_in_dim(block, 0, width, axis=dim), axis, backward)
        block = jnp.concatenate([low, block, high], axis=dim)
    return block


def normalize(values, gain_table):
    token_count = values.shape[0]
    head_count, head_size = gain_table.shape
    split = values.astype(jnp.float32).reshape(token_count, head_count, head_size)
    mean_square = jnp.mean(split * split, axis=-1, keepdims=True)
    return (split * lax.rsqrt(mean_square + EPSILON) * gain_table).astype(jnp.bfloat16)


def layer_terms(queries, key_rows, value_rows, score_scale):
    scores = (
        jnp.einsum("qhd,khd->hqk", queries, key_rows, preferred_element_type=jnp.float32)
        * score_scale
    )
    layer_max = jnp.max(scores, axis=-1)
    unnormed = jnp.exp(scores - layer_max[..., None]).astype(jnp.bfloat16)
    layer_sum = jnp.sum(unnormed.astype(jnp.float32), axis=-1)
    weighted = jnp.einsum("hqk,khd->qhd", unnormed, value_rows, preferred_element_type=jnp.float32)
    return (layer_max, layer_sum, weighted)


def combine(maxima, layer_sums, weighted, presence):
    mask = presence[:, None, None]
    maxima = jnp.where(mask, maxima, NEGATIVE_FLOOR)
    layer_sums = jnp.where(mask, layer_sums, 0.0)
    overall = jnp.max(maxima, axis=0)
    factors = jnp.exp(maxima - overall)
    denominator = jnp.sum(factors * layer_sums, axis=0)
    numerator = jnp.sum(jnp.transpose(factors, (0, 2, 1))[..., None] * weighted, axis=0)
    return numerator / jnp.transpose(denominator)[..., None]


def body(stream, query_input, key_input, value_input, q_gain, k_gain, out_weight, gate):
    token_count, feature_count = query_input.shape
    head_count, head_size = q_gain.shape
    score_scale = 1.0 / math.sqrt(head_size)
    queries = normalize(query_input, q_gain)
    normed_keys = normalize(key_input, k_gain).reshape(token_count, feature_count)
    layered = jnp.stack([normed_keys, value_input], axis=0)[None, None]
    padded = padded_2(layered, (("seq", 0), ("row", 1)), 1)
    padded = padded.reshape(9, 2, token_count, feature_count)
    key_stack = padded[:, 0].reshape(9, token_count, head_count, head_size)
    value_stack = padded[:, 1].reshape(9, token_count, head_count, head_size)
    time_index = lax.axis_index("seq")
    time_count = lax.axis_size("seq")
    height_index = lax.axis_index("row")
    height_count = lax.axis_size("row")
    time_present = [time_index > 0, time_index >= 0, time_index < time_count - 1]
    height_present = [height_index > 0, height_index >= 0, height_index < height_count - 1]
    presence = jnp.stack(
        [time_flag & height_flag for time_flag in time_present for height_flag in height_present]
    )
    result_set = [
        layer_terms(queries, key_stack[layer_index], value_stack[layer_index], score_scale)
        for layer_index in range(9)
    ]
    maxima = jnp.stack([entry[0] for entry in result_set])
    layer_sums = jnp.stack([entry[1] for entry in result_set])
    weighted = jnp.stack([entry[2] for entry in result_set])
    attention = (
        combine(maxima, layer_sums, weighted, presence)
        .reshape(token_count, feature_count)
        .astype(jnp.bfloat16)
    )
    all_heads = lax.all_gather(attention, "col", axis=1, tiled=True)
    projected = jnp.dot(
        all_heads,
        lax.all_gather(out_weight, "row", axis=0, tiled=True),
        preferred_element_type=jnp.float32,
    )
    return (stream.astype(jnp.float32) + gate * projected).astype(jnp.bfloat16)


ABSENT = 1e30
LOG2_E = 1.4426950408889634
MIB = 1 << 20
CUT = 3
FIRST_VMEM = 60 * MIB
LAST_VMEM = 16 * MIB


def vmem_spec():
    return pl.BlockSpec(memory_space=pltpu.VMEM)


def hbm_spec():
    return pl.BlockSpec(memory_space=pltpu.HBM)


def normed(ref, gain_ref, part, out):
    head_size = gain_ref.shape[1]
    half = out.shape[1]
    count = half // head_size
    for index in range(count):
        start = pl.multiple_of(part * half + index * head_size, head_size)
        x = ref[:, pl.ds(start, head_size)].astype(jnp.float32)
        mean_square = jnp.mean(x * x, axis=-1, keepdims=True)
        gain = gain_ref[pl.ds(part * count + index, 1), :]
        scaled = x * lax.rsqrt(mean_square + EPSILON) * gain
        out[:, index * head_size : (index + 1) * head_size] = scaled.astype(jnp.bfloat16)


def prep_kernel(
    k_hbm, v_hbm, kg_hbm, w_hbm, kv_send, kvw_keep, k_ref, kg_ref, sems
):
    mine = lax.axis_index("seq")
    half = kv_send.shape[1] // 2
    rows = pl.ds(pl.multiple_of(mine * half, half), half)
    moved = [(kg_hbm, kg_ref), (k_hbm, k_ref)]
    for part, out in ((1 - mine, kv_send), (mine, kvw_keep)):
        moved.append((v_hbm.at[:, pl.ds(pl.multiple_of(part * half, half), half)], out.at[:, half : 2 * half]))
    moved.append((w_hbm.at[rows, :], kvw_keep.at[:, 2 * half :]))
    copies = [
        pltpu.make_async_copy(source, target, sems.at[index]) for index, (source, target) in enumerate(moved)
    ]
    for copy in copies:
        copy.start()

    copies[0].wait()
    copies[1].wait()
    for part, kv_out in ((1 - mine, kv_send), (mine, kvw_keep)):
        normed(k_ref, kg_ref, part, kv_out.at[:, :half])
    for copy in copies[2:]:
        copy.wait()


def query_kernel(q_hbm, qg_hbm, q_send, q_keep, q_ref, qg_ref, sems):
    mine = lax.axis_index("seq")
    copies = [
        pltpu.make_async_copy(qg_hbm, qg_ref, sems.at[0]),
        pltpu.make_async_copy(q_hbm, q_ref, sems.at[1]),
    ]
    for copy in copies:
        copy.start()
    for copy in copies:
        copy.wait()
    for part, q_out in ((1 - mine, q_send), (mine, q_keep)):
        normed(q_ref, qg_ref, part, q_out)


def prep(q, k, v, q_gain, k_gain, out_weight):
    rows, width = q.shape
    half = width // 2
    one = jax.ShapeDtypeStruct((rows, half), jnp.bfloat16)
    two = jax.ShapeDtypeStruct((rows, width), jnp.bfloat16)
    four = jax.ShapeDtypeStruct((rows, width + out_weight.shape[1]), jnp.bfloat16)
    block = pltpu.VMEM((rows, width), jnp.bfloat16)
    gain = pltpu.VMEM(q_gain.shape, jnp.float32)
    params = pltpu.CompilerParams(vmem_limit_bytes=FIRST_VMEM)
    cost = pl.CostEstimate(flops=rows * width * 8, bytes_accessed=rows * width * 6, transcendentals=0)
    kv_send, kvw = pl.pallas_call(
        prep_kernel,
        out_shape=[two, four],
        in_specs=[hbm_spec()] * 4,
        out_specs=[vmem_spec()] * 2,
        scratch_shapes=[block, gain, pltpu.SemaphoreType.DMA((5,))],
        compiler_params=params,
        cost_estimate=cost,
    )(k, v, k_gain, out_weight)
    kvw, q = lax.optimization_barrier((kvw, q))
    q_send, q_keep = pl.pallas_call(
        query_kernel,
        out_shape=[one, one],
        in_specs=[hbm_spec()] * 2,
        out_specs=[vmem_spec()] * 2,
        scratch_shapes=[block, gain, pltpu.SemaphoreType.DMA((2,))],
        compiler_params=pltpu.CompilerParams(vmem_limit_bytes=LAST_VMEM),
        cost_estimate=cost,
    )(q, q_gain)
    return kv_send, kvw, q_send, q_keep


def attend_kernel(scale, first, head_size, times, *refs):
    queries, refs = refs[: len(times)], refs[len(times) :]
    kv0, kv1, kv2 = refs[:3]
    refs = refs[3:]
    height = lax.axis_index("row")
    flags = [None, None, (height > 0) & (height < lax.axis_size("row") - 1)]
    rows, half = queries[0].shape
    factor = scale * LOG2_E
    ones = jnp.ones((rows, head_size), jnp.bfloat16)

    for index in range(queries[0].shape[1] // head_size):
        columns = slice(index * head_size, (index + 1) * head_size)
        beside = slice(half + index * head_size, half + (index + 1) * head_size)
        keys = [kv[:, columns] for kv in (kv0, kv1, kv2)]
        values = [jnp.concatenate([kv[:, beside], ones], axis=1) for kv in (kv0, kv1, kv2)]
        for which, q_ref in zip(times, queries):
            q = q_ref[:, columns]
            scores = [
                lax.dot_general(q, key, (((1,), (1,)), ((), ())), preferred_element_type=jnp.float32)
                for key in keys
            ]
            top = None
            for flag, score in zip(flags, scores):
                part = score[:, :head_size]
                for start in range(head_size, rows, head_size):
                    part = jnp.maximum(part, score[:, start : start + head_size])
                if flag is not None:
                    part = jnp.where(flag, part, NEGATIVE_FLOOR)
                top = part if top is None else jnp.maximum(top, part)
            top = jnp.max(top, axis=1, keepdims=True)
            total = None
            if not first:
                m_in, acc_in = refs[:2]
                before = m_in[index, which][:, :1]
                top = jnp.maximum(before, top)
                total = acc_in[index, which] * jnp.exp2((before - top) * factor)
            for flag, score, value in zip(flags, scores, values):
                shift = top if flag is None else jnp.where(flag, top, ABSENT)
                weights = jnp.exp2((score - shift) * factor).astype(jnp.bfloat16)
                term = jnp.dot(weights, value, preferred_element_type=jnp.float32)
                total = term if total is None else total + term
            if first:
                m_out, acc_out = refs
                m_out[index, which] = jnp.broadcast_to(top, (rows, head_size))
                acc_out[index, which] = total
            else:
                out = refs[2]
                out[:, columns] = (total[:, :head_size] / total[:, head_size:]).astype(jnp.bfloat16)


def attend(times, queries, layers, head_size, carry=None):
    rows, width = queries[0].shape
    heads = width // head_size
    vmem = pl.BlockSpec(memory_space=pltpu.VMEM)
    arguments = [*queries, *layers]
    if carry is None:
        out_shape = [
            jax.ShapeDtypeStruct((heads, 2, rows, head_size), jnp.float32),
            jax.ShapeDtypeStruct((heads, 2, rows, 2 * head_size), jnp.float32),
        ]
        out_specs = [vmem, vmem]
    else:
        arguments += list(carry)
        out_shape = jax.ShapeDtypeStruct((rows, width), jnp.bfloat16)
        out_specs = vmem
    return pl.pallas_call(
        functools.partial(attend_kernel, 1.0 / math.sqrt(head_size), carry is None, head_size, times),
        out_shape=out_shape,
        in_specs=[vmem] * len(arguments),
        out_specs=out_specs,
        compiler_params=pltpu.CompilerParams(vmem_limit_bytes=16 * MIB),
        cost_estimate=pl.CostEstimate(
            flops=heads * len(times) * rows * 3 * rows * head_size * 8,
            bytes_accessed=8 * MIB,
            transcendentals=heads * len(times) * rows * 3 * rows,
        ),
    )(*arguments)


def plane_sum(pieces, weights, spans, write):
    shift = lax.axis_index("row") ^ lax.axis_index("col")
    for case in range(4):

        @pl.when(shift == case)
        def _(case=case):
            for part, (low, high) in enumerate(spans):
                total = None
                for index, piece in enumerate(pieces):
                    term = jnp.dot(piece, weights(index ^ case, part, low, high), preferred_element_type=jnp.float32)
                    total = term if total is None else total + term
                write(part, low, high, total)


def weight_of(kvw, kvw_pair, kvw_mid, inner, forward, outer, which, low, high):
    start = kvw.shape[1] - kvw.shape[0] * 2
    columns = slice(start + low, start + high)
    if which == 2:
        return inner + forward
    if which == 3:
        return kvw_mid[:, columns] + outer
    return (kvw, kvw_pair)[which][:, columns]


def peer_kernel(span, a0, a1, a2, a3, kvw, kvw_pair, kvw_mid, inner, forward, outer, out):
    def write(part, low, high, total):
        out[...] = total.astype(out.dtype)

    def weights(which, part, low, high):
        held = inner[...], forward[...], outer[...]
        return weight_of(kvw, kvw_pair, kvw_mid, *held, which, low, high)

    plane_sum([a[...] for a in (a0, a1, a2, a3)], weights, [span], write)


def own_kernel(spans, a0, a1, a2, a3, kvw, kvw_pair, kvw_mid, gate, stream_hbm, *rest):
    forward, outer, inner = rest[:2], rest[2:4], rest[4:-3]
    out, stream, sem = rest[-3:]
    copy = pltpu.make_async_copy(stream_hbm, stream, sem)
    copy.start()
    copy.wait()

    def write(part, low, high, total):
        out[:, low:high] = stream[:, low:high].astype(jnp.float32) + gate[:, low:high] * total

    def weights(which, part, low, high):
        held = inner[part][...], forward[part][...], outer[part][...]
        return weight_of(kvw, kvw_pair, kvw_mid, *held, which, low, high)

    plane_sum([a[...] for a in (a0, a1, a2, a3)], weights, spans, write)


def final_kernel(spans, base, gate, *rest):
    received, out_hbm, out, sems = rest[:-3], rest[-3], rest[-2], rest[-1]
    copies = []
    for part, (low, high) in enumerate(spans):
        total = base[:, low:high] + gate[:, low:high] * received[part][...].astype(jnp.float32)
        out[:, low:high] = total.astype(out.dtype)
        copies.append(pltpu.make_async_copy(out.at[:, low:high], out_hbm.at[:, low:high], sems.at[part]))
        copies[-1].start()
    for copy in copies:
        copy.wait()


def pair_body(stream, query_input, key_input, value_input, q_gain, k_gain, out_weight, gate):
    head_size = q_gain.shape[1]
    tokens, width = stream.shape
    rows = lax.axis_size("row")
    cut = width // 6 * CUT
    spans = [(0, cut), (cut, width)]

    def swap(x):
        return lax.ppermute(x, "seq", [(0, 1), (1, 0)])

    def pair(x):
        return lax.ppermute(x, "row", [(i, i ^ 1) for i in range(4)])

    def middle(x):
        return lax.ppermute(x, "row", [(1, 2), (2, 1)])

    def along(x, axis, mask):
        return lax.ppermute(x, axis, [(i, i ^ mask) for i in range(4)])

    def call(kernel, arguments, specs, out_shape, out_spec, scratch, flops):
        return pl.pallas_call(
            kernel,
            out_shape=out_shape,
            in_specs=specs,
            out_specs=out_spec,
            scratch_shapes=scratch,
            compiler_params=pltpu.CompilerParams(vmem_limit_bytes=LAST_VMEM),
            cost_estimate=pl.CostEstimate(flops=flops, bytes_accessed=2 * MIB, transcendentals=0),
        )(*arguments)

    def inward(x):
        return lax.ppermute(x, "row", [(1, 0), (2, 3)])

    barrier = lax.optimization_barrier
    kv_send, kvw, q_send, q_keep = prep(query_input, key_input, value_input, q_gain, k_gain, out_weight)
    kv_peer = swap(kv_send)
    kvw_pair, kvw_mid = pair(kvw), middle(kvw)
    q_peer = swap(q_send)
    peer_pair, peer_mid = pair(kv_peer), middle(kv_peer)

    carry = attend((0, 1), [q_keep, q_peer], [kvw, kvw_pair, kvw_mid], head_size)
    starts = [width + low for low, high in spans] + [2 * width]
    halves = [slice(starts[part], starts[part + 1]) for part in range(2)]
    first_pair, early_mid, carry = barrier((kvw_pair[:, halves[0]], kvw_mid[:, halves[0]], carry))
    inner, forwards = [inward(early_mid)], [middle(first_pair)]
    layers = [kv_peer, peer_pair, peer_mid]
    theirs = attend((1,), [q_peer], layers, head_size, carry)
    across_theirs, beside_theirs = along(theirs, "col", 2), along(theirs, "col", 1)
    next_pair, next_mid, _ = barrier((kvw_pair[:, halves[1]], kvw_mid[:, halves[1]], theirs))
    forwards.append(middle(next_pair))
    inner.append(inward(next_mid))
    outer = [inward(forwards[part]) for part in range(2)]

    gate = gate.reshape(1, width)
    vmem, hbm = vmem_spec(), hbm_spec()
    groups = [theirs, beside_theirs, across_theirs, along(across_theirs, "col", 1)]
    sents = []
    for part, (low, high) in enumerate(spans):
        sent = call(
            functools.partial(peer_kernel, (low, high)),
            [*groups, kvw, kvw_pair, kvw_mid, inner[part], forwards[part], outer[part]],
            [vmem] * 10,
            jax.ShapeDtypeStruct((tokens, high - low), jnp.bfloat16),
            vmem,
            [],
            tokens * width * (high - low) * 40,
        )
        if part == 0:
            sent, groups[0] = barrier((sent, groups[0]))
        sents.append(sent)
    received = [swap(sent) for sent in sents]
    carry, forwards[1], inner[0] = barrier((carry, forwards[1], inner[0]))
    mine = attend((0,), [q_keep], layers, head_size, carry)
    beside_mine = along(mine, "col", 1)
    across_mine = along(mine, "col", 2)
    groups = [mine, beside_mine, across_mine, along(beside_mine, "col", 2)]
    base = call(
        functools.partial(own_kernel, spans),
        [*groups, kvw, kvw_pair, kvw_mid, gate, stream, *forwards, *outer, *inner],
        [vmem] * 8 + [hbm] + [vmem] * (4 + len(inner)),
        jax.ShapeDtypeStruct((tokens, width), jnp.float32),
        vmem,
        [pltpu.VMEM((tokens, width), stream.dtype), pltpu.SemaphoreType.DMA(())],
        tokens * width * width * 4,
    )
    return call(
        functools.partial(final_kernel, spans),
        [base, gate, *received],
        [vmem] * (2 + len(received)),
        jax.ShapeDtypeStruct((tokens, width), jnp.bfloat16),
        hbm,
        [pltpu.VMEM((tokens, width), jnp.bfloat16), pltpu.SemaphoreType.DMA((len(spans),))],
        tokens * width * 4,
    )


def solution(mesh):
    placed = (
        P(("seq", "row"), "col"),
        P(("seq", "row"), "col"),
        P(("seq", "row"), "col"),
        P(("seq", "row"), "col"),
        P("col", None),
        P("col", None),
        P("row", "col"),
        P("col"),
    )
    shape = mesh.shape
    paired = shape["seq"] == 2 and shape["row"] == 4 and shape["col"] == 4
    return jax.shard_map(
        pair_body if paired else body, mesh=mesh, in_specs=placed, out_specs=P(("seq", "row"), "col"), check_vma=False
    )
```
